768 devices in a mesh: gx: 8 (over y_lo, core), gy: 96 (over y_hi, z, x).
Axes of the slice: x: 4, y: 8 (y_hi: 2, y_lo: 4; y = y_hi * 4 + y_lo), z: 12, core: 2. Of those that a mesh axis runs over, the one named last changes fastest.
Arguments:
- positions: float32 [3, 8, 96, 512], P(None, 'gx', 'gy'), may hold values from 0 to 32, as said below
- species: int32 [8, 96, 512], P('gx', 'gy'), may hold values from 0 to 4
- send_index: int32 [8, 96, 384], P('gx', 'gy'), may hold values from 0 to 511, as said below
- edge_centers: int32 [8, 96, 512], P('gx', 'gy'), may hold values from 0 to 511, as said below
- edge_neighbours: int32 [8, 96, 512], P('gx', 'gy'), may hold values from 0 to 3967, as said below
- block_counts: int32 [8, 96, 4], P('gx', 'gy'), may hold values from 1 to 128, as said below
- emb_center: float32 [5, 128], replicated, may hold values from -5 to 5
- emb_neighbour: float32 [5, 128], replicated, may hold values from -5 to 5
- radial_w: float32 [8, 128], replicated, may hold values from -2 to 2
- env_w: float32 [2, 128, 128], replicated, may hold values from -0.5 to 0.5
- mix_w: float32 [2, 128, 128], replicated, may hold values from -0.5 to 0.5
- out_w: float32 [128], replicated, may hold values from -0.5 to 0.5
Outputs:
- forces: float32 [3, 8, 96, 512], P(None, 'gx', 'gy')
- grad_mix: float32 [2, 128, 128], replicated
- grad_out: float32 [128], replicated
- mean_energy: float32 [], replicated
The draws below stay inside these ranges and needn't reach their ends.
Inputs may be any that keep to these rules, and one draw needn't show every extreme that they name: `positions`: each atom lies within its device's block; every edge's neighbour lies within 6 of its centre in the pool's coordinates. `send_index`: within one block the 384 entries are distinct atoms, in rising order: those within two lattice columns of the block's four side faces. `edge_centers`: within one block the centres are non-decreasing along the edge slots. `edge_neighbours`: pool index into the block's pool; slot 4 (the block itself) is never named: the value lies in [0, 512) or in [512 + s * 384, 512 + (s + 1) * 384) with s != 4; it never names the centre itself. `block_counts`: the first edge block of every device is full.
All inputs are finite; a program needn't handle non-finite values.
Results may differ from the reference program's by a relative error of at most 0.0003.
Values sent between devices are 32-bit elements; how exact they have to be, the bound alone decides.
No kernel may reach another device: no remote copies, remote signals or barrier semaphores. Data moves between devices by JAX's collectives and lax.ppermute only.
A program may use at most 32 MiB of HBM per device.

```python
import jax
import jax.numpy as jnp
import numpy as np
from jax import lax

CHANNELS = 128
SPECIES = 5
RADIAL = 8
LAYERS = 2
BLOCK_EDGES = 128
LAT = 8
DEPTH = 8
EDGE_BLOCKS = 4
A_DEV = 512
EXPORT = 384
EDGES = 512
GRID_X = 8
GRID_Y = 96


SPACING = 1.7


Z_SPACING = 3.4


JITTER = 0.3


def offset_table():
    rows = []
    for di in range(-2, 3):
        for dj in range(-2, 3):
            if di != 0 or dj != 0:
                rows.append((di, dj, 0))
    for dk in (-1, 1):
        for di in range(-1, 2):
            for dj in range(-1, 2):
                rows.append((di, dj, dk))
    return np.array(rows, dtype=np.int32)


def lattice_layout(key):
    keys = jax.random.split(jax.random.fold_in(key, 21), GRID_X * GRID_Y)
    site_of = jax.vmap(lambda k: jax.random.permutation(k, A_DEV))(keys)
    site_of = site_of.reshape(GRID_X, GRID_Y, A_DEV).astype(jnp.int32)
    atom_at = jnp.argsort(site_of, axis=-1).astype(jnp.int32)
    site_i = site_of // (LAT * DEPTH)
    site_j = site_of // DEPTH % LAT
    site_k = site_of % DEPTH
    rim = ((site_i < 2) | (site_i >= LAT - 2) | (site_j < 2) | (site_j >= LAT - 2)).astype(jnp.int32)
    rank = (jnp.cumsum(rim, axis=-1) - 1).astype(jnp.int32)
    return (site_of, atom_at, site_i, site_j, site_k, rim, rank)


def draw_positions(key, part):
    site_of, atom_at, site_i, site_j, site_k, rim, rank = lattice_layout(key)
    base = jnp.stack([site_i.astype(jnp.float32) * SPACING + 0.5 * SPACING, site_j.astype(jnp.float32) * SPACING + 0.5 * SPACING, site_k.astype(jnp.float32) * Z_SPACING + 0.5 * Z_SPACING])
    jkey = jax.random.fold_in(key, 22)
    jitter = jax.random.uniform(jkey, base.shape, jnp.float32, -JITTER, JITTER)
    return (base + jitter).astype(jnp.float32)


def draw_send_index(key, part):
    site_of, atom_at, site_i, site_j, site_k, rim, rank = lattice_layout(key)
    order = jnp.argsort(1 - rim, axis=-1, stable=True)
    return order[..., :EXPORT].astype(jnp.int32)


def draw_edge_centers(key, part):
    keys = jax.random.split(jax.random.fold_in(key, 12), GRID_X * GRID_Y)
    rows = jax.vmap(lambda k: jnp.sort(jax.random.randint(k, (EDGES,), 0, A_DEV)))(keys)
    return rows.reshape(GRID_X, GRID_Y, EDGES).astype(jnp.int32)


def draw_edge_neighbours(key, part):
    site_of, atom_at, site_i, site_j, site_k, rim, rank = lattice_layout(key)
    centers = draw_edge_centers(key, part)
    ci = jnp.take_along_axis(site_i, centers, axis=-1)
    cj = jnp.take_along_axis(site_j, centers, axis=-1)
    ck = jnp.take_along_axis(site_k, centers, axis=-1)
    table = jnp.array(offset_table())
    pick = jax.random.randint(jax.random.fold_in(key, 13), centers.shape, 0, table.shape[0])
    step = table[pick]
    ti = ci + step[..., 0]
    tj = cj + step[..., 1]
    tk = ck + step[..., 2]
    tk = jnp.where((tk < 0) | (tk >= DEPTH), ck - step[..., 2], tk)
    slot_a = 1 + (ti >= LAT).astype(jnp.int32) - (ti < 0).astype(jnp.int32)
    slot_b = 1 + (tj >= LAT).astype(jnp.int32) - (tj < 0).astype(jnp.int32)
    target = (ti % LAT * LAT + tj % LAT) * DEPTH + tk
    grid_x = jnp.arange(GRID_X, dtype=jnp.int32)[:, None, None]
    grid_y = jnp.arange(GRID_Y, dtype=jnp.int32)[None, :, None]
    owner_x = (grid_x + slot_a - 1) % GRID_X
    owner_y = (grid_y + slot_b - 1) % GRID_Y
    owner_atom = atom_at[owner_x, owner_y, target]
    owner_rank = rank[owner_x, owner_y, owner_atom]
    local = (slot_a == 1) & (slot_b == 1)
    ghost = A_DEV + (3 * slot_a + slot_b) * EXPORT + owner_rank
    return jnp.where(local, owner_atom, ghost).astype(jnp.int32)


def draw_block_counts(key, part):
    keys = jax.random.split(jax.random.fold_in(key, 14), 3)
    live = jax.random.randint(keys[0], (GRID_X, GRID_Y, 1), 1, EDGE_BLOCKS + 1)
    dense = jax.random.randint(keys[1], (GRID_X, GRID_Y, EDGE_BLOCKS), 64, BLOCK_EDGES + 1)
    sparse = jax.random.randint(keys[2], (GRID_X, GRID_Y, EDGE_BLOCKS), 1, 33)
    blocks = jnp.arange(EDGE_BLOCKS)[None, None, :]
    counts = jnp.where(blocks < live, dense, sparse)
    counts = counts.at[:, :, 0].set(BLOCK_EDGES)
    return counts.astype(jnp.int32)


def with_ends(values, rng, low, high):
    longest = values.shape.index(max(values.shape))
    spots = []
    for shift in (0, 1):
        where = [jax.random.randint(jax.random.fold_in(rng, axis), (), 0, length) for axis, length in enumerate(values.shape)]
        where[longest] = (where[longest] + shift) % values.shape[longest]
        spots.append(tuple(where))
    return values.at[spots[0]].set(low).at[spots[1]].set(high)


def normal_values(rng, dims, width, most, kind=jnp.bfloat16):
    return jnp.clip(width * jax.random.normal(rng, dims, jnp.float32), -most, most).astype(kind)


def setup_inputs(seed: int = 0) -> dict:
    key_list = jax.random.split(jax.random.key(seed), 13)
    positions = draw_positions(jax.random.fold_in(key_list[12], 71), 0)
    species = with_ends(jax.random.randint(key_list[1], (GRID_X, GRID_Y, A_DEV), 0, SPECIES), jax.random.fold_in(key_list[1], 1), 0, SPECIES - 1).astype(jnp.int32)
    send_index = draw_send_index(jax.random.fold_in(key_list[12], 71), 0)
    edge_centers = draw_edge_centers(jax.random.fold_in(key_list[12], 71), 0)
    edge_neighbours = draw_edge_neighbours(jax.random.fold_in(key_list[12], 71), 0)
    block_counts = draw_block_counts(jax.random.fold_in(key_list[12], 71), 0)
    emb_center = normal_values(key_list[6], (SPECIES, CHANNELS), 1.0, 5.0, jnp.float32)
    emb_neighbour = normal_values(key_list[7], (SPECIES, CHANNELS), 1.0, 5.0, jnp.float32)
    radial_w = normal_values(key_list[8], (RADIAL, CHANNELS), RADIAL ** -0.5, 2.0, jnp.float32)
    env_w = normal_values(key_list[9], (LAYERS, CHANNELS, CHANNELS), CHANNELS ** -0.5, 0.5, jnp.float32)
    mix_w = normal_values(key_list[10], (LAYERS, CHANNELS, CHANNELS), CHANNELS ** -0.5, 0.5, jnp.float32)
    out_w = normal_values(key_list[11], (CHANNELS,), CHANNELS ** -0.5, 0.5, jnp.float32)
    return dict(positions=positions, species=species, send_index=send_index, edge_centers=edge_centers, edge_neighbours=edge_neighbours, block_counts=block_counts, emb_center=emb_center, emb_neighbour=emb_neighbour, radial_w=radial_w, env_w=env_w, mix_w=mix_w, out_w=out_w)


CUTOFF = 6.0
SOFTENING = 0.25
SPACING = 1.7
PRECISE = lax.Precision.HIGHEST

def device_energy(own_pos, ghost_pos, ghost_species, own_species, centers, neighbours, counts, emb_center, emb_neighbour, radial_w, env_w, mix_w, out_w):
    block_side = SPACING * LAT
    ghost_total = ghost_pos.shape[1]
    atom_count = own_pos.shape[1]
    per_slot = ghost_total // 9
    slot_ids = jnp.arange(ghost_total) // per_slot
    shift_x = (slot_ids // 3 - 1).astype(jnp.float32) * block_side
    shift_y = (slot_ids % 3 - 1).astype(jnp.float32) * block_side
    offset = jnp.stack([shift_x, shift_y, jnp.zeros_like(shift_x)])
    pool_pos = jnp.concatenate([own_pos, ghost_pos + offset], axis=1)
    pool_species = jnp.concatenate([own_species, ghost_species])
    edge_total = centers.shape[0]
    offset_vec = pool_pos[:, neighbours] - own_pos[:, centers]
    radius = jnp.sqrt(lax.optimization_barrier(jnp.sum(offset_vec * offset_vec, axis=0)) + SOFTENING)
    unit_vec = offset_vec / radius
    ratio = radius / CUTOFF
    smooth = (1.0 - ratio * ratio) ** 2
    slot_in_block = jnp.arange(edge_total) % BLOCK_EDGES
    block_of = jnp.arange(edge_total) // BLOCK_EDGES
    live_mask = (slot_in_block < counts[block_of]).astype(jnp.float32)
    orders = jnp.arange(1, radial_w.shape[0] + 1).astype(jnp.float32)
    radial_basis = jnp.sin(orders[None, :] * jnp.pi * radius[:, None] / CUTOFF) / radius[:, None]
    kinds = jnp.arange(emb_center.shape[0]).astype(jnp.float32)
    centre_hot = (own_species[centers][:, None] == kinds[None, :]).astype(jnp.float32)
    neighbour_hot = (pool_species[neighbours][:, None] == kinds[None, :]).astype(jnp.float32)
    summed = jnp.dot(centre_hot, emb_center, precision=PRECISE)
    summed = summed + jnp.dot(neighbour_hot, emb_neighbour, precision=PRECISE)
    summed = summed + jnp.dot(radial_basis, radial_w, precision=PRECISE)
    latent = jax.nn.silu(summed) * smooth[:, None]
    for layer in range(env_w.shape[0]):
        weighted = jnp.dot(latent, env_w[layer], precision=PRECISE) * live_mask[:, None]
        back = jnp.zeros_like(latent)
        for comp in range(3):
            environ = jax.ops.segment_sum(weighted * unit_vec[comp][:, None], centers, num_segments=atom_count, indices_are_sorted=True)
            back = back + environ[centers] * unit_vec[comp][:, None]
        coupled = latent * back
        latent = latent + jax.nn.silu(jnp.dot(coupled, mix_w[layer], precision=PRECISE))
    readout = jnp.dot(latent, out_w, precision=PRECISE)
    return jnp.sum(live_mask * smooth * readout)

def reference(positions, species, send_index, edge_centers, edge_neighbours, block_counts, emb_center, emb_neighbour, radial_w, env_w, mix_w, out_w):
    device_total = GRID_X * GRID_Y
    atom_count = positions.shape[3]
    per_slot = send_index.shape[2]
    species_f = species.astype(jnp.float32)

    def total(positions, mix_w, out_w):
        exported_pos = jnp.take_along_axis(positions, send_index[None], axis=3)
        exported_species = jnp.take_along_axis(species_f, send_index, axis=2)
        exported = jnp.concatenate([exported_pos, exported_species[None]], axis=0)
        slots = []
        for row in range(3):
            for col in range(3):
                slots.append(jnp.roll(exported, (1 - row, 1 - col), axis=(1, 2)))
        ghosts = jnp.stack(slots, axis=0)
        ghosts = jnp.transpose(ghosts, (2, 3, 1, 0, 4)).reshape(device_total, 4, 9 * per_slot)
        own_all = jnp.transpose(positions, (1, 2, 0, 3)).reshape(device_total, 3, atom_count)
        species_all = species_f.reshape(device_total, atom_count)
        centers_all = edge_centers.reshape(device_total, -1)
        neighbours_all = edge_neighbours.reshape(device_total, -1)
        counts_all = block_counts.reshape(device_total, -1)

        def one_device(items):
            own_pos, ghost, own_species, centers, neighbours, counts = items
            return device_energy(own_pos, ghost[:3], ghost[3], own_species, centers, neighbours, counts, emb_center, emb_neighbour, radial_w, env_w, mix_w, out_w)
        energies = lax.map(jax.checkpoint(one_device), (own_all, ghosts, species_all, centers_all, neighbours_all, counts_all))
        return jnp.sum(energies)
    energy, grads = jax.value_and_grad(total, argnums=(0, 1, 2))(positions, mix_w, out_w)
    scale = jnp.float32(device_total)
    return (-grads[0], grads[1] / scale, grads[2] / scale, energy / scale)
```

```python
import math

import jax
import jax.numpy as jnp
from jax import lax
from jax.experimental import pallas as pl
from jax.experimental.pallas import tpu as pltpu
from jax.sharding import Mesh
from jax.sharding import PartitionSpec as P

BLOCK_EDGES = 128
LAT = 8
CUTOFF = 6.0
SOFTENING = 0.25
SPACING = 1.7
LANES = 128

GX = ("gx_0", "gx_1")
GY = ("gy_0", "gy_1", "gy_2")
ALL = GX + GY
NEAR = ("gx_1", "gy_2")
MIDDLE = ("gx_0", "gy_0")
FAR = ("gy_1",)

F32 = jnp.float32
BF16 = jnp.bfloat16
NN = ((1,), (0,))
NT = ((1,), (1,))
TN = ((0,), (0,))


def iota(shape, dim):
    return lax.broadcasted_iota(jnp.int32, shape, dim)


def bdot(a, b, dims):
    return lax.dot_general(a, b, (dims, ((), ())), preferred_element_type=F32)


def split2(x):
    hi = x.astype(BF16)
    return hi, (x - hi.astype(F32)).astype(BF16)


def split3(x):
    hi = x.astype(BF16).astype(F32)
    rest = x - hi
    mid = rest.astype(BF16).astype(F32)
    return hi, mid, rest - mid


def mm(a, b, dims):
    return bdot(a[0], b[0], dims) + (bdot(a[0], b[1], dims) + bdot(a[1], b[0], dims))


def mm6(a, b, dims):
    small = bdot(a[0], b[2], dims) + bdot(a[1], b[1], dims) + bdot(a[2], b[0], dims)
    return bdot(a[0], b[0], dims) + (bdot(a[0], b[1], dims) + bdot(a[1], b[0], dims) + small)


def thirds(x):
    return tuple(part.astype(BF16) for part in split3(x))


def sigmoid(x):
    return 1.0 / (1.0 + jnp.exp(-x))


def export_kernel(pos_ref, spec_ref, send_ref, out_ref):
    atoms, count = pos_ref.shape[3], send_ref.shape[2]
    rows = [pos_ref[c, 0] for c in range(3)] + [spec_ref[0].astype(F32)]
    table = jnp.concatenate(rows, axis=0)
    parts = jnp.concatenate(split3(table) + (jnp.zeros_like(table),), axis=0).astype(BF16)
    hot = (iota((atoms, count), 0) == send_ref[0]).astype(F32).astype(BF16)
    found = bdot(parts, hot, NN)
    found = (found[0:4] + found[4:8]) + found[8:12]
    out_ref[...] = jnp.zeros_like(out_ref)
    for j in range(count // LANES):
        for c in range(4):
            out_ref[j : j + 1, c * LANES : (c + 1) * LANES] = found[c : c + 1, j * LANES : (j + 1) * LANES]


def main_kernel(
    counts_ref,
    pos_ref,
    spec_ref,
    x0_ref,
    x2_ref,
    y0_ref,
    y2_ref,
    cent_ref,
    neigh_ref,
    embc_ref,
    embn_ref,
    radw_ref,
    envw_ref,
    mixw_ref,
    outw_ref,
    own_ref,
    a0_ref,
    a1_ref,
    a2_ref,
    pack_ref,
    q_ref,
    w_ref,
    *,
    blocks,
    devices,
):
    atoms = pos_ref.shape[3]
    edges = cent_ref.shape[2]
    own_rows = atoms // LANES
    side = SPACING * LAT

    for c in range(4):
        row = pos_ref[c, 0] if c < 3 else spec_ref[0].astype(F32)
        for h in range(own_rows):
            q_ref[h : h + 1, c * LANES : (c + 1) * LANES] = row[:, h * LANES : (h + 1) * LANES]
    lane = iota((4, 4 * LANES), 1)
    for s in range(9):
        a, b = s // 3, s % 3
        rows = slice(own_rows + 4 * s, own_rows + 4 * s + 4)
        if s == 4:
            q_ref[rows, :] = jnp.zeros((4, 4 * LANES), F32)
            continue
        ghost = (y0_ref[a], None, y2_ref[a])[b] if b != 1 else (x0_ref, x2_ref)[a // 2][...]
        shift = jnp.where(lane < LANES, F32((a - 1) * side), jnp.where(lane < 2 * LANES, F32((b - 1) * side), 0.0))
        q_ref[rows, :] = ghost + shift
    total_rows = q_ref.shape[0]

    ends = jnp.concatenate([neigh_ref[0], cent_ref[0]], axis=1)
    at_row = iota((total_rows, 2 * edges), 0)
    past = at_row - own_rows
    holds = jnp.where(past < 0, at_row, jnp.where(past % 4 == 3, -1, own_rows + 3 * (past // 4) + past % 4))
    hot = (holds == ends // LANES).astype(F32)
    in_lane = iota((LANES, 2 * edges), 0) == ends % LANES
    table = jnp.concatenate(split3(q_ref[...]), axis=0).astype(BF16)
    hot3 = jnp.concatenate([hot, hot, hot], axis=0).astype(BF16)
    runs = bdot(table, hot3, TN)
    picked = [
        jnp.sum(jnp.where(in_lane, runs[c * LANES : (c + 1) * LANES], 0.0), axis=0, keepdims=True) for c in range(4)
    ]

    dist = [p[:, :edges] - p[:, edges:] for p in picked[:3]]
    radius = jnp.sqrt((dist[0] * dist[0] + dist[1] * dist[1] + dist[2] * dist[2]) + SOFTENING)
    inverse = 1.0 / radius
    unit = [d * inverse for d in dist]
    ratio = radius * (1.0 / CUTOFF)
    gap = 1.0 - ratio * ratio
    smooth = gap * gap
    edge = iota((1, edges), 1)
    limit = jnp.full((1, edges), counts_ref[0, 0, 0], jnp.int32)
    for k in range(1, blocks):
        limit = jnp.where(edge >= k * BLOCK_EDGES, counts_ref[0, 0, k], limit)
    live = (edge % BLOCK_EDGES < limit).astype(F32)
    order = (iota((8, edges), 0) + 1).astype(F32) * F32(math.pi / CUTOFF)
    angle = order * radius
    sines, cosines = jnp.sin(angle), jnp.cos(angle)
    basis = sines * inverse
    slope = (order * cosines - basis) * inverse
    kind = iota((8, edges), 0).astype(F32)
    features = jnp.concatenate(
        [
            basis,
            (kind == picked[3][:, edges:]).astype(F32),
            (kind == picked[3][:, :edges]).astype(F32),
        ],
        axis=0,
    )
    species = embc_ref.shape[0]
    w_ref[...] = jnp.zeros_like(w_ref)
    w_ref[0:8, :] = radw_ref[...]
    w_ref[8 : 8 + species, :] = embc_ref[...]
    w_ref[16 : 16 + species, :] = embn_ref[...]

    centre = cent_ref[0].astype(F32)
    weight = live * smooth
    zero = jnp.zeros((1, edges), F32)
    columns = jnp.transpose(jnp.concatenate([smooth, weight, live, centre] + [zero] * 4, axis=0))
    smooth_col, weight_col, live_col, centre_col = (columns[:, k : k + 1] for k in range(4))

    units = jnp.concatenate(unit + [zero] * 5, axis=0)
    units_s = split2(units)
    cosine = mm(units_s, units_s, TN)
    same = jnp.logical_and(centre_col == centre, live_col * live > 0.0)
    pairs = split2(jnp.where(same, cosine, 0.0))

    summed = mm6(thirds(features), thirds(w_ref[...]), TN)
    gate0 = sigmoid(summed)
    first = summed * gate0
    latent = first * smooth_col

    layers = envw_ref.shape[0]
    share = 1.0 / devices
    saved = []
    for l in range(layers):
        env_s, mix_s = split2(envw_ref[l]), split2(mixw_ref[l])
        weighted_s = split2(mm(split2(latent), env_s, NN))
        back = mm(pairs, weighted_s, NN)
        coupled_s = split2(latent * back)
        pre = mm(coupled_s, mix_s, NN)
        gate = sigmoid(pre)
        saved.append((env_s, mix_s, weighted_s, latent, back, coupled_s, pre, gate))
        latent = latent + pre * gate

    out_rows = jnp.broadcast_to(outw_ref[...], (8, LANES))
    latent_s = split2(latent)
    readout = mm6(thirds(out_rows), thirds(latent), NT)[0:1]
    energy = jnp.sum(weight * readout, axis=1, keepdims=True)
    grad_out = mm(split2(jnp.concatenate([weight] + [zero] * 7, axis=0)), latent_s, NN)

    dlatent = weight_col * outw_ref[...]
    dpairs = None
    for l in reversed(range(layers)):
        env_s, mix_s, weighted_s, latent, back, coupled_s, pre, gate = saved[l]
        dpre_s = split2(dlatent * (gate * (1.0 + pre * (1.0 - gate))))
        pack_ref[l * LANES : (l + 1) * LANES, :] = mm(coupled_s, dpre_s, TN) * share
        dcoupled = mm(dpre_s, mix_s, NT)
        dback_s = split2(dcoupled * latent)
        term = mm(dback_s, weighted_s, NT)
        dpairs = term if dpairs is None else dpairs + term
        dweighted_s = split2(mm(pairs, dback_s, NN))
        dlatent = dlatent + dcoupled * back + mm(dweighted_s, env_s, NT)
    rest = pack_ref.shape[0] - layers * LANES
    row = iota((rest, LANES), 0)
    tail = jnp.where(row == 0, grad_out[0:1], jnp.where(row == 1, energy, 0.0))
    pack_ref[layers * LANES :, :] = tail * share

    dpairs_s = split2(jnp.where(same, dpairs, 0.0))
    dunits = mm(units_s, dpairs_s, NT) + mm(units_s, dpairs_s, NN)
    dfirst = dlatent * first
    dsmooth = live * readout + mm(split2(jnp.ones((8, LANES), F32)), split2(dfirst), NT)[0:1]
    dsummed = dlatent * smooth_col * (gate0 * (1.0 + summed * (1.0 - gate0)))
    dbasis = mm(split2(w_ref[0:8, :]), split2(dsummed), NT)
    dradius = jnp.sum(dbasis * slope, axis=0, keepdims=True) - dsmooth * (gap * radius * F32(4.0 / CUTOFF**2))
    along = dunits[0:1] * unit[0] + dunits[1:2] * unit[1] + dunits[2:3] * unit[2]
    radial = dradius - along * inverse
    moves = []
    for c in range(3):
        push = dunits[c : c + 1] * inverse + unit[c] * radial
        moves.append(jnp.where(in_lane, jnp.concatenate([push, -push], axis=1), 0.0))
    moves = split3(jnp.concatenate(moves, axis=0))
    hot_b = hot.astype(BF16)
    pool = (bdot(hot_b, moves[0].astype(BF16), NT) + bdot(hot_b, moves[1].astype(BF16), NT)) + bdot(
        hot_b, moves[2].astype(BF16), NT
    )
    own_ref[...] = pool[0:own_rows]
    for s in range(9):
        rows = slice(own_rows + 4 * s, own_rows + 4 * s + 4)
        (a0_ref, a1_ref, a2_ref)[s // 3][s % 3] = pool[rows]


def force_kernel(send_ref, own_ref, down_ref, up_ref, left_ref, right_ref, out_ref):
    atoms, count = out_ref.shape[3], send_ref.shape[2]
    back = (down_ref[1] + up_ref[1]) + (left_ref[...] + right_ref[...])
    rows = []
    for c in range(3):
        lanes = slice(c * LANES, (c + 1) * LANES)
        rows.append(jnp.concatenate([back[j : j + 1, lanes] for j in range(count // LANES)], axis=1))
    rows.append(jnp.zeros((1, count), F32))
    values = jnp.concatenate(rows, axis=0)
    parts = jnp.concatenate(split3(values) + (jnp.zeros_like(values),), axis=0).astype(BF16)
    hot = (iota((atoms, count), 0) == send_ref[0]).astype(F32).astype(BF16)
    placed = bdot(parts, hot, NT)
    placed = (placed[0:4] + placed[4:8]) + placed[8:12]
    own = own_ref[...]
    for c in range(3):
        lanes = slice(c * LANES, (c + 1) * LANES)
        mine = jnp.concatenate([own[h : h + 1, lanes] for h in range(atoms // LANES)], axis=1)
        out_ref[c, 0] = -(mine + placed[c : c + 1])


def passed_along(block, axis, distance):
    count = lax.axis_size(axis)
    route = [((i - distance) % count, i) for i in range(count)]
    return lax.ppermute(block, axis, route)


def exchanged(shard, axes):
    return lax.all_to_all(shard, axes, 0, 0)


def summed_over(shard, axes):
    copies = jnp.broadcast_to(shard[None], (lax.axis_size(axes),) + shard.shape)
    return jnp.sum(exchanged(copies, axes), axis=0)


def summed_over_all(pack):
    near = lax.axis_size(NEAR)
    rows = pack.shape[0] // near
    part = jnp.sum(exchanged(pack.reshape(near, rows, LANES), NEAR), axis=0)
    part = summed_over(summed_over(part, MIDDLE), FAR)
    copies = jnp.broadcast_to(part[None], (near, rows, LANES))
    return exchanged(copies, NEAR).reshape(near * rows, LANES)


def body(
    positions,
    species,
    send_index,
    edge_centers,
    edge_neighbours,
    block_counts,
    emb_center,
    emb_neighbour,
    radial_w,
    env_w,
    mix_w,
    out_w,
):
    atoms = positions.shape[3]
    edges = edge_centers.shape[2]
    layers = env_w.shape[0]
    own_rows = atoms // LANES
    devices = lax.axis_size(ALL)
    tiles = 8 * lax.axis_size(NEAR)
    packed = (layers * LANES + 2 + tiles - 1) // tiles * tiles
    vmem = pl.BlockSpec(memory_space=pltpu.VMEM)

    exported = pl.pallas_call(
        export_kernel,
        out_shape=jax.ShapeDtypeStruct((4, 4 * LANES), F32),
        in_specs=[vmem] * 3,
        out_specs=vmem,
        name="export",
    )(positions, species, send_index)

    x0 = passed_along(exported, GX, 1)
    x2 = passed_along(exported, GX, -1)
    column = jnp.stack([x0, exported, x2])
    y0 = passed_along(column, GY, 1)
    y2 = passed_along(column, GY, -1)

    piece = jax.ShapeDtypeStruct((3, 4, 3 * LANES), F32)
    own, a0, a1, a2, pack = pl.pallas_call(
        lambda *refs: main_kernel(*refs, blocks=edges // BLOCK_EDGES, devices=devices),
        out_shape=(
            jax.ShapeDtypeStruct((own_rows, 3 * LANES), F32),
            piece,
            piece,
            piece,
            jax.ShapeDtypeStruct((packed, LANES), F32),
        ),
        in_specs=[pl.BlockSpec(memory_space=pltpu.SMEM)] + [vmem] * 14,
        out_specs=(vmem,) * 5,
        scratch_shapes=[
            pltpu.VMEM((own_rows + 36, 4 * LANES), F32),
            pltpu.VMEM((24, LANES), F32),
        ],
        name="edges",
    )(
        block_counts,
        positions,
        species,
        x0,
        x2,
        y0,
        y2,
        edge_centers,
        edge_neighbours,
        emb_center,
        emb_neighbour,
        radial_w,
        env_w,
        mix_w,
        out_w.reshape(1, LANES),
    )

    down = passed_along(a0, GX, -1)
    up = passed_along(a2, GX, 1)
    left = passed_along(a1[0] + down[0] + up[0], GY, -1)
    right = passed_along(a1[2] + down[2] + up[2], GY, 1)
    forces = pl.pallas_call(
        force_kernel,
        out_shape=jax.ShapeDtypeStruct(positions.shape, F32),
        in_specs=[vmem] * 6,
        out_specs=vmem,
        name="forces",
    )(send_index, own, down, up, left, right)

    total = summed_over_all(pack)
    top = layers * LANES
    return forces, total[:top].reshape(layers, LANES, LANES), total[top], total[top + 1, 0]


def solution(mesh):
    finer = Mesh(mesh.devices.reshape(4, 2, 2, 12, 4), ALL)
    sharded = P(GX, GY, None)
    placed = (P(None, GX, GY, None),) + (sharded,) * 5 + (P(),) * 6
    return jax.shard_map(
        body,
        mesh=finer,
        in_specs=placed,
        out_specs=(P(None, GX, GY, None), P(), P(), P()),
        check_vma=False,
    )
```

```python
import math

import jax
import jax.numpy as jnp
from jax import lax
from jax.experimental import pallas as pl
from jax.experimental.pallas import tpu as pltpu
from jax.sharding import Mesh
from jax.sharding import PartitionSpec as P

BLOCK_EDGES = 128
LAT = 8
CUTOFF = 6.0
SOFTENING = 0.25
SPACING = 1.7
LANES = 128

GX = ("gx_0", "gx_1")
GY = ("gy_0", "gy_1", "gy_2")
ALL = GX + GY
NEAR = ("gx_1", "gy_2")
MIDDLE = ("gx_0", "gy_0")
FAR = ("gy_1",)

F32 = jnp.float32
BF16 = jnp.bfloat16
NN = ((1,), (0,))
NT = ((1,), (1,))
TN = ((0,), (0,))


def iota(shape, dim):
    return lax.broadcasted_iota(jnp.int32, shape, dim)


def bdot(a, b, dims):
    return lax.dot_general(a, b, (dims, ((), ())), preferred_element_type=F32)


def split2(x):
    hi = x.astype(BF16)
    return hi, (x - hi.astype(F32)).astype(BF16)


def split3(x):
    hi = x.astype(BF16).astype(F32)
    rest = x - hi
    mid = rest.astype(BF16).astype(F32)
    return hi, mid, rest - mid


def mm(a, b, dims):
    return bdot(a[0], b[0], dims) + (bdot(a[0], b[1], dims) + bdot(a[1], b[0], dims))


def mm6(a, b, dims):
    small = bdot(a[0], b[2], dims) + bdot(a[1], b[1], dims) + bdot(a[2], b[0], dims)
    return bdot(a[0], b[0], dims) + (bdot(a[0], b[1], dims) + bdot(a[1], b[0], dims) + small)


def thirds(x):
    return tuple(part.astype(BF16) for part in split3(x))


def sigmoid(x):
    return 1.0 / (1.0 + jnp.exp(-x))


def export_kernel(pos_ref, spec_ref, send_ref, out_ref):
    atoms, count = pos_ref.shape[3], send_ref.shape[2]
    rows = [pos_ref[c, 0] for c in range(3)] + [spec_ref[0].astype(F32)]
    table = jnp.concatenate(rows, axis=0)
    parts = jnp.concatenate(split3(table) + (jnp.zeros_like(table),), axis=0).astype(BF16)
    hot = (iota((atoms, count), 0) == send_ref[0]).astype(F32).astype(BF16)
    found = bdot(parts, hot, NN)
    found = (found[0:4] + found[4:8]) + found[8:12]
    out_ref[...] = jnp.zeros_like(out_ref)
    for j in range(count // LANES):
        for c in range(4):
            out_ref[j : j + 1, c * LANES : (c + 1) * LANES] = found[c : c + 1, j * LANES : (j + 1) * LANES]


def main_kernel(
    counts_ref,
    pos_ref,
    spec_ref,
    x0_ref,
    x2_ref,
    y0_ref,
    y2_ref,
    cent_ref,
    neigh_ref,
    embc_ref,
    embn_ref,
    radw_ref,
    outw_ref,
    envw_hbm,
    mixw_hbm,
    own_ref,
    a0_ref,
    a1_ref,
    a2_ref,
    pack_ref,
    q_ref,
    w_ref,
    envw_ref,
    mixw_ref,
    sems,
    *,
    blocks,
    devices,
):
    loads = [
        pltpu.make_async_copy(envw_hbm, envw_ref, sems.at[0]),
        pltpu.make_async_copy(mixw_hbm, mixw_ref, sems.at[1]),
    ]
    for load in loads:
        load.start()
    atoms = pos_ref.shape[3]
    edges = cent_ref.shape[2]
    own_rows = atoms // LANES
    side = SPACING * LAT

    for c in range(4):
        row = pos_ref[c, 0] if c < 3 else spec_ref[0].astype(F32)
        for h in range(own_rows):
            q_ref[h : h + 1, c * LANES : (c + 1) * LANES] = row[:, h * LANES : (h + 1) * LANES]
    lane = iota((4, 4 * LANES), 1)
    for s in range(9):
        a, b = s // 3, s % 3
        rows = slice(own_rows + 4 * s, own_rows + 4 * s + 4)
        if s == 4:
            q_ref[rows, :] = jnp.zeros((4, 4 * LANES), F32)
            continue
        ghost = (y0_ref[a], None, y2_ref[a])[b] if b != 1 else (x0_ref, x2_ref)[a // 2][...]
        shift = jnp.where(lane < LANES, F32((a - 1) * side), jnp.where(lane < 2 * LANES, F32((b - 1) * side), 0.0))
        q_ref[rows, :] = ghost + shift
    total_rows = q_ref.shape[0]

    ends = jnp.concatenate([neigh_ref[0], cent_ref[0]], axis=1)
    at_row = iota((total_rows, 2 * edges), 0)
    past = at_row - own_rows
    holds = jnp.where(past < 0, at_row, jnp.where(past % 4 == 3, -1, own_rows + 3 * (past // 4) + past % 4))
    hot = (holds == ends // LANES).astype(F32)
    in_lane = iota((LANES, 2 * edges), 0) == ends % LANES
    table = jnp.concatenate(split3(q_ref[...]), axis=0).astype(BF16)
    hot3 = jnp.concatenate([hot, hot, hot], axis=0).astype(BF16)
    runs = bdot(table, hot3, TN)
    picked = [
        jnp.sum(jnp.where(in_lane, runs[c * LANES : (c + 1) * LANES], 0.0), axis=0, keepdims=True) for c in range(4)
    ]

    dist = [p[:, :edges] - p[:, edges:] for p in picked[:3]]
    radius = jnp.sqrt((dist[0] * dist[0] + dist[1] * dist[1] + dist[2] * dist[2]) + SOFTENING)
    inverse = 1.0 / radius
    unit = [d * inverse for d in dist]
    ratio = radius * (1.0 / CUTOFF)
    gap = 1.0 - ratio * ratio
    smooth = gap * gap
    edge = iota((1, edges), 1)
    limit = jnp.full((1, edges), counts_ref[0, 0, 0], jnp.int32)
    for k in range(1, blocks):
        limit = jnp.where(edge >= k * BLOCK_EDGES, counts_ref[0, 0, k], limit)
    live = (edge % BLOCK_EDGES < limit).astype(F32)
    order = (iota((8, edges), 0) + 1).astype(F32) * F32(math.pi / CUTOFF)
    angle = order * radius
    sines, cosines = jnp.sin(angle), jnp.cos(angle)
    basis = sines * inverse
    slope = (order * cosines - basis) * inverse
    kind = iota((8, edges), 0).astype(F32)
    features = jnp.concatenate(
        [
            basis,
            (kind == picked[3][:, edges:]).astype(F32),
            (kind == picked[3][:, :edges]).astype(F32),
        ],
        axis=0,
    )
    species = embc_ref.shape[0]
    w_ref[...] = jnp.zeros_like(w_ref)
    w_ref[0:8, :] = radw_ref[...]
    w_ref[8 : 8 + species, :] = embc_ref[...]
    w_ref[16 : 16 + species, :] = embn_ref[...]

    centre = cent_ref[0].astype(F32)
    weight = live * smooth
    zero = jnp.zeros((1, edges), F32)
    columns = jnp.transpose(jnp.concatenate([smooth, weight, live, centre] + [zero] * 4, axis=0))
    smooth_col, weight_col, live_col, centre_col = (columns[:, k : k + 1] for k in range(4))

    units = jnp.concatenate(unit + [zero] * 5, axis=0)
    units_s = split2(units)
    cosine = mm(units_s, units_s, TN)
    same = jnp.logical_and(centre_col == centre, live_col * live > 0.0)
    pairs = split2(jnp.where(same, cosine, 0.0))

    summed = mm6(thirds(features), thirds(w_ref[...]), TN)
    gate0 = sigmoid(summed)
    first = summed * gate0
    latent = first * smooth_col

    for load in loads:
        load.wait()
    layers = envw_ref.shape[0]
    chunk = layers * LANES // pack_ref.shape[0]
    share = 1.0 / devices
    saved = []
    for l in range(layers):
        env_s, mix_s = split2(envw_ref[l]), split2(mixw_ref[l])
        weighted_s = split2(mm(split2(latent), env_s, NN))
        back = mm(pairs, weighted_s, NN)
        coupled_s = split2(latent * back)
        pre = mm(coupled_s, mix_s, NN)
        gate = sigmoid(pre)
        saved.append((env_s, mix_s, weighted_s, latent, back, coupled_s, pre, gate))
        latent = latent + pre * gate

    out_rows = jnp.broadcast_to(outw_ref[...], (8, LANES))
    latent_s = split2(latent)
    readout = mm6(thirds(out_rows), thirds(latent), NT)[0:1]
    energy = jnp.sum(weight * readout, axis=1, keepdims=True)
    grad_out = mm(split2(jnp.concatenate([weight] + [zero] * 7, axis=0)), latent_s, NN)

    dlatent = weight_col * outw_ref[...]
    dpairs = None
    for l in reversed(range(layers)):
        env_s, mix_s, weighted_s, latent, back, coupled_s, pre, gate = saved[l]
        dpre_s = split2(dlatent * (gate * (1.0 + pre * (1.0 - gate))))
        grad_mix = mm(coupled_s, dpre_s, TN) * share
        step = min(chunk, LANES)
        for k in range(0, LANES, step):
            place, start = divmod(l * LANES + k, chunk)
            pack_ref[place, start : start + step, :] = grad_mix[k : k + step]
        dcoupled = mm(dpre_s, mix_s, NT)
        dback_s = split2(dcoupled * latent)
        term = mm(dback_s, weighted_s, NT)
        dpairs = term if dpairs is None else dpairs + term
        dweighted_s = split2(mm(pairs, dback_s, NN))
        dlatent = dlatent + dcoupled * back + mm(dweighted_s, env_s, NT)
    row = iota((8, LANES), 0)
    tail = jnp.where(row == 0, grad_out[0:1], jnp.where(row == 1, energy, 0.0)) * share
    for k in range(pack_ref.shape[0]):
        pack_ref[k, chunk:, :] = tail

    dpairs_s = split2(jnp.where(same, dpairs, 0.0))
    dunits = mm(units_s, dpairs_s, NT) + mm(units_s, dpairs_s, NN)
    dfirst = dlatent * first
    dsmooth = live * readout + mm(split2(jnp.ones((8, LANES), F32)), split2(dfirst), NT)[0:1]
    dsummed = dlatent * smooth_col * (gate0 * (1.0 + summed * (1.0 - gate0)))
    dbasis = mm(split2(w_ref[0:8, :]), split2(dsummed), NT)
    dradius = jnp.sum(dbasis * slope, axis=0, keepdims=True) - dsmooth * (gap * radius * F32(4.0 / CUTOFF**2))
    along = dunits[0:1] * unit[0] + dunits[1:2] * unit[1] + dunits[2:3] * unit[2]
    radial = dradius - along * inverse
    moves = []
    for c in range(3):
        push = dunits[c : c + 1] * inverse + unit[c] * radial
        moves.append(jnp.where(in_lane, jnp.concatenate([push, -push], axis=1), 0.0))
    moves = split3(jnp.concatenate(moves, axis=0))
    hot_b = hot.astype(BF16)
    pool = (bdot(hot_b, moves[0].astype(BF16), NT) + bdot(hot_b, moves[1].astype(BF16), NT)) + bdot(
        hot_b, moves[2].astype(BF16), NT
    )
    own_ref[...] = pool[0:own_rows]
    for s in range(9):
        rows = slice(own_rows + 4 * s, own_rows + 4 * s + 4)
        (a0_ref, a1_ref, a2_ref)[s // 3][s % 3] = pool[rows]


def force_kernel(send_ref, own_ref, down_ref, up_ref, left_ref, right_ref, out_ref):
    atoms, count = out_ref.shape[3], send_ref.shape[2]
    back = (down_ref[1] + up_ref[1]) + (left_ref[...] + right_ref[...])
    rows = []
    for c in range(3):
        lanes = slice(c * LANES, (c + 1) * LANES)
        rows.append(jnp.concatenate([back[j : j + 1, lanes] for j in range(count // LANES)], axis=1))
    rows.append(jnp.zeros((1, count), F32))
    values = jnp.concatenate(rows, axis=0)
    parts = jnp.concatenate(split3(values) + (jnp.zeros_like(values),), axis=0).astype(BF16)
    hot = (iota((atoms, count), 0) == send_ref[0]).astype(F32).astype(BF16)
    placed = bdot(parts, hot, NT)
    placed = (placed[0:4] + placed[4:8]) + placed[8:12]
    own = own_ref[...]
    for c in range(3):
        lanes = slice(c * LANES, (c + 1) * LANES)
        mine = jnp.concatenate([own[h : h + 1, lanes] for h in range(atoms // LANES)], axis=1)
        out_ref[c, 0] = -(mine + placed[c : c + 1])


def passed_along(block, axis, distance):
    count = lax.axis_size(axis)
    route = [((i - distance) % count, i) for i in range(count)]
    return lax.ppermute(block, axis, route)


def exchanged(shard, axes):
    return lax.all_to_all(shard, axes, 0, 0)


def summed_over(shard, axes):
    copies = jnp.broadcast_to(shard[None], (lax.axis_size(axes),) + shard.shape)
    return jnp.sum(exchanged(copies, axes), axis=0)


def body(
    positions,
    species,
    send_index,
    edge_centers,
    edge_neighbours,
    block_counts,
    emb_center,
    emb_neighbour,
    radial_w,
    env_w,
    mix_w,
    out_w,
):
    atoms = positions.shape[3]
    edges = edge_centers.shape[2]
    layers = env_w.shape[0]
    own_rows = atoms // LANES
    devices = lax.axis_size(ALL)
    near = lax.axis_size(NEAR)
    chunk = layers * LANES // near
    vmem = pl.BlockSpec(memory_space=pltpu.VMEM)

    def near_by(*arrays):
        return [pltpu.with_memory_space_constraint(a, pltpu.VMEM) for a in arrays]

    def result(*shape):
        return pltpu.VMEM(shape, F32)

    exported = pl.pallas_call(
        export_kernel,
        out_shape=result(4, 4 * LANES),
        in_specs=[vmem] * 3,
        out_specs=vmem,
        name="export",
    )(positions, species, send_index)

    x0 = passed_along(exported, GX, 1)
    x2 = passed_along(exported, GX, -1)
    column = jnp.stack([x0, exported, x2])
    y0 = passed_along(column, GY, 1)
    y2 = passed_along(column, GY, -1)

    piece = result(3, 4, 3 * LANES)
    own, a0, a1, a2, pack = pl.pallas_call(
        lambda *refs: main_kernel(*refs, blocks=edges // BLOCK_EDGES, devices=devices),
        out_shape=(
            result(own_rows, 3 * LANES),
            piece,
            piece,
            piece,
            result(near, chunk + 8, LANES),
        ),
        in_specs=[pl.BlockSpec(memory_space=pltpu.SMEM)] + [vmem] * 12 + [pl.BlockSpec(memory_space=pl.ANY)] * 2,
        out_specs=(vmem,) * 5,
        scratch_shapes=[
            pltpu.VMEM((own_rows + 36, 4 * LANES), F32),
            pltpu.VMEM((24, LANES), F32),
            pltpu.VMEM(env_w.shape, F32),
            pltpu.VMEM(mix_w.shape, F32),
            pltpu.SemaphoreType.DMA((2,)),
        ],
        name="edges",
    )(
        block_counts,
        *near_by(
            positions,
            species,
            x0,
            x2,
            y0,
            y2,
            edge_centers,
            edge_neighbours,
            emb_center,
            emb_neighbour,
            radial_w,
            out_w.reshape(1, LANES),
        ),
        env_w,
        mix_w,
    )

    down = passed_along(a0, GX, -1)
    up = passed_along(a2, GX, 1)
    part = jnp.sum(exchanged(pack, NEAR), axis=0)
    part, down, up = lax.optimization_barrier((part, down, up))
    part = summed_over(part, MIDDLE)
    left = passed_along(a1[0] + down[0] + up[0], GY, -1)
    right = passed_along(a1[2] + down[2] + up[2], GY, 1)
    part = summed_over(part, FAR)
    part, left, right = lax.optimization_barrier((part, left, right))
    forces = pl.pallas_call(
        force_kernel,
        out_shape=jax.ShapeDtypeStruct(positions.shape, F32),
        in_specs=[vmem] * 6,
        out_specs=vmem,
        name="forces",
    )(send_index, *near_by(own, down, up, left, right))
    shared = jnp.broadcast_to(part[None, :chunk], (near, chunk, LANES))
    grad_mix = exchanged(shared, NEAR).reshape(layers, LANES, LANES)
    return forces, grad_mix, part[chunk], part[chunk + 1, 0]


def solution(mesh):
    finer = Mesh(mesh.devices.reshape(4, 2, 2, 12, 4), ALL)
    sharded = P(GX, GY, None)
    placed = (P(None, GX, GY, None),) + (sharded,) * 5 + (P(),) * 6
    return jax.shard_map(
        body,
        mesh=finer,
        in_specs=placed,
        out_specs=(P(None, GX, GY, None), P(), P(), P()),
        check_vma=False,
    )
```

```python
import math

import jax
import jax.numpy as jnp
from jax import lax
from jax.experimental import pallas as pl
from jax.experimental.pallas import tpu as pltpu
from jax.sharding import Mesh
from jax.sharding import PartitionSpec as P

BLOCK_EDGES = 128
LAT = 8
CUTOFF = 6.0
SOFTENING = 0.25
SPACING = 1.7
LANES = 128

GX = ("gx_0", "gx_1")
GY = ("gy_0", "gy_1", "gy_2")
ALL = GX + GY
NEAR = ("gx_1", "gy_2")
MIDDLE = ("gx_0", "gy_0")
FAR = ("gy_1",)

F32 = jnp.float32
BF16 = jnp.bfloat16
NN = ((1,), (0,))
NT = ((1,), (1,))
TN = ((0,), (0,))


def iota(shape, dim):
    return lax.broadcasted_iota(jnp.int32, shape, dim)


def bdot(a, b, dims):
    return lax.dot_general(a, b, (dims, ((), ())), preferred_element_type=F32)


def split2(x):
    hi = x.astype(BF16)
    return hi, (x - hi.astype(F32)).astype(BF16)


def split3(x):
    hi = x.astype(BF16).astype(F32)
    rest = x - hi
    mid = rest.astype(BF16).astype(F32)
    return hi, mid, rest - mid


def mm(a, b, dims):
    return bdot(a[0], b[0], dims) + (bdot(a[0], b[1], dims) + bdot(a[1], b[0], dims))


def mm6(a, b, dims):
    small = bdot(a[0], b[2], dims) + bdot(a[1], b[1], dims) + bdot(a[2], b[0], dims)
    return bdot(a[0], b[0], dims) + (bdot(a[0], b[1], dims) + bdot(a[1], b[0], dims) + small)


def thirds(x):
    return tuple(part.astype(BF16) for part in split3(x))


def sigmoid(x):
    return 1.0 / (1.0 + jnp.exp(-x))


def export_kernel(pos_ref, spec_ref, send_ref, out_ref):
    atoms, count = pos_ref.shape[3], send_ref.shape[2]
    rows = [pos_ref[c, 0] for c in range(3)] + [spec_ref[0].astype(F32)]
    table = jnp.concatenate(rows, axis=0)
    parts = jnp.concatenate(split3(table) + (jnp.zeros_like(table),), axis=0).astype(BF16)
    hot = (iota((atoms, count), 0) == send_ref[0]).astype(F32).astype(BF16)
    found = bdot(parts, hot, NN)
    found = (found[0:4] + found[4:8]) + found[8:12]
    out_ref[...] = jnp.zeros_like(out_ref)
    for j in range(count // LANES):
        for c in range(4):
            out_ref[j : j + 1, c * LANES : (c + 1) * LANES] = found[c : c + 1, j * LANES : (j + 1) * LANES]


def main_kernel(
    side_ref,
    counts_ref,
    pos_ref,
    spec_ref,
    xa_ref,
    xb_ref,
    ya_ref,
    yb_ref,
    cent_ref,
    neigh_ref,
    embc_ref,
    embn_ref,
    radw_ref,
    outw_ref,
    envw_hbm,
    mixw_hbm,
    own_ref,
    a0_ref,
    a1_ref,
    a2_ref,
    pack_ref,
    q_ref,
    w_ref,
    envw_ref,
    mixw_ref,
    sems,
    *,
    blocks,
    devices,
):
    loads = [
        pltpu.make_async_copy(envw_hbm, envw_ref, sems.at[0]),
        pltpu.make_async_copy(mixw_hbm, mixw_ref, sems.at[1]),
    ]
    for load in loads:
        load.start()
    atoms = pos_ref.shape[3]
    edges = cent_ref.shape[2]
    own_rows = atoms // LANES
    side = SPACING * LAT

    for c in range(4):
        row = pos_ref[c, 0] if c < 3 else spec_ref[0].astype(F32)
        for h in range(own_rows):
            q_ref[h : h + 1, c * LANES : (c + 1) * LANES] = row[:, h * LANES : (h + 1) * LANES]
    turn_x = 2 * (side_ref[0] // 2) - 1
    turn_y = 2 * (side_ref[0] % 2) - 1
    lane = iota((4, 4 * LANES), 1)
    for s in range(9):
        a, b = s // 3, s % 3
        rows = slice(own_rows + 4 * s, own_rows + 4 * s + 4)
        if s == 4:
            q_ref[rows, :] = jnp.zeros((4, 4 * LANES), F32)
            continue
        ghost = (ya_ref[a], None, yb_ref[a])[b] if b != 1 else (xa_ref, xb_ref)[a // 2][...]
        shift_x = (turn_x * (a - 1)).astype(F32) * F32(side)
        shift_y = (turn_y * (b - 1)).astype(F32) * F32(side)
        q_ref[rows, :] = ghost + jnp.where(lane < LANES, shift_x, jnp.where(lane < 2 * LANES, shift_y, 0.0))
    total_rows = q_ref.shape[0]

    ends = jnp.concatenate([neigh_ref[0], cent_ref[0]], axis=1)
    at_row = iota((total_rows, 2 * edges), 0)
    past = at_row - own_rows
    slot = 3 * (1 + turn_x * (past // 12 - 1)) + 1 + turn_y * (past // 4 % 3 - 1)
    holds = jnp.where(past < 0, at_row, jnp.where(past % 4 == 3, -1, own_rows + 3 * slot + past % 4))
    hot = (holds == ends // LANES).astype(F32)
    in_lane = iota((LANES, 2 * edges), 0) == ends % LANES
    table = jnp.concatenate(split3(q_ref[...]), axis=0).astype(BF16)
    hot3 = jnp.concatenate([hot, hot, hot], axis=0).astype(BF16)
    runs = bdot(table, hot3, TN)
    picked = [
        jnp.sum(jnp.where(in_lane, runs[c * LANES : (c + 1) * LANES], 0.0), axis=0, keepdims=True) for c in range(4)
    ]

    dist = [p[:, :edges] - p[:, edges:] for p in picked[:3]]
    radius = jnp.sqrt((dist[0] * dist[0] + dist[1] * dist[1] + dist[2] * dist[2]) + SOFTENING)
    inverse = 1.0 / radius
    unit = [d * inverse for d in dist]
    ratio = radius * (1.0 / CUTOFF)
    gap = 1.0 - ratio * ratio
    smooth = gap * gap
    edge = iota((1, edges), 1)
    limit = jnp.full((1, edges), counts_ref[0, 0, 0], jnp.int32)
    for k in range(1, blocks):
        limit = jnp.where(edge >= k * BLOCK_EDGES, counts_ref[0, 0, k], limit)
    live = (edge % BLOCK_EDGES < limit).astype(F32)
    order = (iota((8, edges), 0) + 1).astype(F32) * F32(math.pi / CUTOFF)
    angle = order * radius
    sines, cosines = jnp.sin(angle), jnp.cos(angle)
    basis = sines * inverse
    slope = (order * cosines - basis) * inverse
    kind = iota((8, edges), 0).astype(F32)
    features = jnp.concatenate(
        [
            basis,
            (kind == picked[3][:, edges:]).astype(F32),
            (kind == picked[3][:, :edges]).astype(F32),
        ],
        axis=0,
    )
    species = embc_ref.shape[0]
    w_ref[...] = jnp.zeros_like(w_ref)
    w_ref[0:8, :] = radw_ref[...]
    w_ref[8 : 8 + species, :] = embc_ref[...]
    w_ref[16 : 16 + species, :] = embn_ref[...]

    centre = cent_ref[0].astype(F32)
    weight = live * smooth
    zero = jnp.zeros((1, edges), F32)
    columns = jnp.transpose(jnp.concatenate([smooth, weight, live, centre] + [zero] * 4, axis=0))
    smooth_col, weight_col, live_col, centre_col = (columns[:, k : k + 1] for k in range(4))

    units = jnp.concatenate(unit + [zero] * 5, axis=0)
    units_s = split2(units)
    cosine = mm(units_s, units_s, TN)
    same = jnp.logical_and(centre_col == centre, live_col * live > 0.0)
    pairs = split2(jnp.where(same, cosine, 0.0))

    summed = mm6(thirds(features), thirds(w_ref[...]), TN)
    gate0 = sigmoid(summed)
    first = summed * gate0
    latent = first * smooth_col

    for load in loads:
        load.wait()
    layers = envw_ref.shape[0]
    chunk = layers * LANES // pack_ref.shape[0]
    share = 1.0 / devices
    saved = []
    for l in range(layers):
        env_s, mix_s = split2(envw_ref[l]), split2(mixw_ref[l])
        weighted_s = split2(mm(split2(latent), env_s, NN))
        back = mm(pairs, weighted_s, NN)
        coupled_s = split2(latent * back)
        pre = mm(coupled_s, mix_s, NN)
        gate = sigmoid(pre)
        saved.append((env_s, mix_s, weighted_s, latent, back, coupled_s, pre, gate))
        latent = latent + pre * gate

    out_rows = jnp.broadcast_to(outw_ref[...], (8, LANES))
    latent_s = split2(latent)
    readout = mm6(thirds(out_rows), thirds(latent), NT)[0:1]
    energy = jnp.sum(weight * readout, axis=1, keepdims=True)
    grad_out = mm(split2(jnp.concatenate([weight] + [zero] * 7, axis=0)), latent_s, NN)

    dlatent = weight_col * outw_ref[...]
    dpairs = None
    for l in reversed(range(layers)):
        env_s, mix_s, weighted_s, latent, back, coupled_s, pre, gate = saved[l]
        dpre_s = split2(dlatent * (gate * (1.0 + pre * (1.0 - gate))))
        grad_mix = mm(coupled_s, dpre_s, TN) * share
        step = min(chunk, LANES)
        for k in range(0, LANES, step):
            place, start = divmod(l * LANES + k, chunk)
            pack_ref[place, start : start + step, :] = grad_mix[k : k + step]
        dcoupled = mm(dpre_s, mix_s, NT)
        dback_s = split2(dcoupled * latent)
        term = mm(dback_s, weighted_s, NT)
        dpairs = term if dpairs is None else dpairs + term
        dweighted_s = split2(mm(pairs, dback_s, NN))
        dlatent = dlatent + dcoupled * back + mm(dweighted_s, env_s, NT)
    row = iota((8, LANES), 0)
    tail = jnp.where(row == 0, grad_out[0:1], jnp.where(row == 1, energy, 0.0)) * share
    for k in range(pack_ref.shape[0]):
        pack_ref[k, chunk:, :] = tail

    dpairs_s = split2(jnp.where(same, dpairs, 0.0))
    dunits = mm(units_s, dpairs_s, NT) + mm(units_s, dpairs_s, NN)
    dfirst = dlatent * first
    dsmooth = live * readout + mm(split2(jnp.ones((8, LANES), F32)), split2(dfirst), NT)[0:1]
    dsummed = dlatent * smooth_col * (gate0 * (1.0 + summed * (1.0 - gate0)))
    dbasis = mm(split2(w_ref[0:8, :]), split2(dsummed), NT)
    dradius = jnp.sum(dbasis * slope, axis=0, keepdims=True) - dsmooth * (gap * radius * F32(4.0 / CUTOFF**2))
    along = dunits[0:1] * unit[0] + dunits[1:2] * unit[1] + dunits[2:3] * unit[2]
    radial = dradius - along * inverse
    moves = []
    for c in range(3):
        push = dunits[c : c + 1] * inverse + unit[c] * radial
        moves.append(jnp.where(in_lane, jnp.concatenate([push, -push], axis=1), 0.0))
    moves = split3(jnp.concatenate(moves, axis=0))
    hot_b = hot.astype(BF16)
    pool = (bdot(hot_b, moves[0].astype(BF16), NT) + bdot(hot_b, moves[1].astype(BF16), NT)) + bdot(
        hot_b, moves[2].astype(BF16), NT
    )
    own_ref[...] = pool[0:own_rows]
    for s in range(9):
        rows = slice(own_rows + 4 * s, own_rows + 4 * s + 4)
        (a0_ref, a1_ref, a2_ref)[s // 3][s % 3] = pool[rows]


def force_kernel(send_ref, own_ref, down_ref, up_ref, left_ref, right_ref, part_ref, out_ref, gout_ref, energy_ref):
    gout_ref[...] = part_ref[0:1, :]
    energy_ref[...] = part_ref[1:2, 0:1]
    atoms, count = out_ref.shape[3], send_ref.shape[2]
    back = (down_ref[1] + up_ref[1]) + (left_ref[...] + right_ref[...])
    rows = []
    for c in range(3):
        lanes = slice(c * LANES, (c + 1) * LANES)
        rows.append(jnp.concatenate([back[j : j + 1, lanes] for j in range(count // LANES)], axis=1))
    rows.append(jnp.zeros((1, count), F32))
    values = jnp.concatenate(rows, axis=0)
    parts = jnp.concatenate(split3(values) + (jnp.zeros_like(values),), axis=0).astype(BF16)
    hot = (iota((atoms, count), 0) == send_ref[0]).astype(F32).astype(BF16)
    placed = bdot(parts, hot, NT)
    placed = (placed[0:4] + placed[4:8]) + placed[8:12]
    own = own_ref[...]
    for c in range(3):
        lanes = slice(c * LANES, (c + 1) * LANES)
        mine = jnp.concatenate([own[h : h + 1, lanes] for h in range(atoms // LANES)], axis=1)
        out_ref[c, 0] = -(mine + placed[c : c + 1])


def traded(block, axis, first):
    count = lax.axis_size(axis)
    route = [(i, (i + 1 if i % 2 == first else i - 1) % count) for i in range(count)]
    return lax.ppermute(block, axis, route)


def exchanged(shard, axes):
    return lax.all_to_all(shard, axes, 0, 0)


def summed_over(shard, axes):
    copies = jnp.broadcast_to(shard[None], (lax.axis_size(axes),) + shard.shape)
    return jnp.sum(exchanged(copies, axes), axis=0)


def body(
    positions,
    species,
    send_index,
    edge_centers,
    edge_neighbours,
    block_counts,
    emb_center,
    emb_neighbour,
    radial_w,
    env_w,
    mix_w,
    out_w,
):
    atoms = positions.shape[3]
    edges = edge_centers.shape[2]
    layers = env_w.shape[0]
    own_rows = atoms // LANES
    devices = lax.axis_size(ALL)
    near = lax.axis_size(NEAR)
    chunk = layers * LANES // near
    vmem = pl.BlockSpec(memory_space=pltpu.VMEM)

    def near_by(*arrays):
        return [pltpu.with_memory_space_constraint(a, pltpu.VMEM) for a in arrays]

    def result(*shape):
        return pltpu.VMEM(shape, F32)

    exported = pl.pallas_call(
        export_kernel,
        out_shape=result(4, 4 * LANES),
        in_specs=[vmem] * 3,
        out_specs=vmem,
        name="export",
    )(positions, species, send_index)

    side = (2 * (lax.axis_index(GX) % 2) + lax.axis_index(GY) % 2).reshape(1)
    xb = traded(exported, GX, 1)
    xa = traded(exported, GX, 0)
    column = jnp.stack([xa, exported, xb])
    yb = traded(column, GY, 1)
    ya = traded(column, GY, 0)

    piece = result(3, 4, 3 * LANES)
    own, a0, a1, a2, pack = pl.pallas_call(
        lambda *refs: main_kernel(*refs, blocks=edges // BLOCK_EDGES, devices=devices),
        out_shape=(
            result(own_rows, 3 * LANES),
            piece,
            piece,
            piece,
            result(near, chunk + 8, LANES),
        ),
        in_specs=[pl.BlockSpec(memory_space=pltpu.SMEM)] * 2 + [vmem] * 12 + [pl.BlockSpec(memory_space=pl.ANY)] * 2,
        out_specs=(vmem,) * 5,
        scratch_shapes=[
            pltpu.VMEM((own_rows + 36, 4 * LANES), F32),
            pltpu.VMEM((24, LANES), F32),
            pltpu.VMEM(env_w.shape, F32),
            pltpu.VMEM(mix_w.shape, F32),
            pltpu.SemaphoreType.DMA((2,)),
        ],
        name="edges",
    )(
        side,
        block_counts,
        *near_by(
            positions,
            species,
            xa,
            xb,
            ya,
            yb,
            edge_centers,
            edge_neighbours,
            emb_center,
            emb_neighbour,
            radial_w,
            out_w.reshape(1, LANES),
        ),
        env_w,
        mix_w,
    )

    over = traded(a2, GX, 1), traded(a0, GX, 0)
    part = jnp.sum(exchanged(pack, NEAR), axis=0)
    part = summed_over(part, MIDDLE)
    part, over = lax.optimization_barrier((part, over))
    across = (
        traded(a1[2] + over[0][2] + over[1][2], GY, 1),
        traded(a1[0] + over[0][0] + over[1][0], GY, 0),
    )
    part = summed_over(part, FAR)
    part, across = lax.optimization_barrier((part, across))
    forces, grad_out, energy = pl.pallas_call(
        force_kernel,
        out_shape=(
            jax.ShapeDtypeStruct(positions.shape, F32),
            jax.ShapeDtypeStruct((1, LANES), F32),
            jax.ShapeDtypeStruct((1, 1), F32),
        ),
        in_specs=[vmem] * 7,
        out_specs=(vmem,) * 3,
        name="forces",
    )(send_index, *near_by(own, *over, *across, part[chunk:]))
    shared = jnp.broadcast_to(part[None, :chunk], (near, chunk, LANES))
    grad_mix = exchanged(shared, NEAR).reshape(layers, LANES, LANES)
    return forces, grad_mix, grad_out.reshape(LANES), energy.reshape(())


def solution(mesh):
    finer = Mesh(mesh.devices.reshape(4, 2, 2, 12, 4), ALL)
    sharded = P(GX, GY, None)
    placed = (P(None, GX, GY, None),) + (sharded,) * 5 + (P(),) * 6
    return jax.shard_map(
        body,
        mesh=finer,
        in_specs=placed,
        out_specs=(P(None, GX, GY, None), P(), P(), P()),
        check_vma=False,
    )
```

```python
import math

import jax
import jax.numpy as jnp
from jax import lax
from jax.experimental import pallas as pl
from jax.experimental.pallas import tpu as pltpu
from jax.sharding import Mesh
from jax.sharding import PartitionSpec as P

BLOCK_EDGES = 128
LAT = 8
CUTOFF = 6.0
SOFTENING = 0.25
SPACING = 1.7
LANES = 128

GX = ("gx_0", "gx_1")
GY = ("gy_0", "gy_1", "gy_2")
ALL = GX + GY
NEAR = ("gx_1", "gy_2")
MIDDLE = ("gx_0", "gy_0")
FAR = ("gy_1",)

F32 = jnp.float32
BF16 = jnp.bfloat16
NN = ((1,), (0,))
NT = ((1,), (1,))
TN = ((0,), (0,))


def iota(shape, dim):
    return lax.broadcasted_iota(jnp.int32, shape, dim)


def bdot(a, b, dims):
    return lax.dot_general(a, b, (dims, ((), ())), preferred_element_type=F32)


def split2(x):
    hi = x.astype(BF16)
    return hi, (x - hi.astype(F32)).astype(BF16)


def split3(x):
    hi = x.astype(BF16).astype(F32)
    rest = x - hi
    mid = rest.astype(BF16).astype(F32)
    return hi, mid, rest - mid


def thirds(x):
    return tuple(part.astype(BF16) for part in split3(x))


def stack(parts, axis):
    return jnp.concatenate([part.astype(F32) for part in parts], axis=axis).astype(BF16)


def halves(out):
    return out[:, :LANES] + out[:, LANES:]


def mm_square(a, b, dims):
    left = jnp.concatenate(a, axis=1)
    if dims == NN:
        row = jnp.concatenate(b, axis=1)
        return halves(bdot(left, jnp.concatenate([row, row], axis=0), NN))
    column = jnp.concatenate(b, axis=0)
    return halves(bdot(left, jnp.concatenate([column, column], axis=1), NT))


def mm_wide(a, b):
    return halves(bdot(a[0], jnp.concatenate(b, axis=1), NN)) + bdot(a[1], b[0], NN)


def mm_turned(a, b):
    out = bdot(jnp.concatenate(a, axis=1), jnp.concatenate(b, axis=1), TN)
    return halves(out[:LANES] + out[LANES:])


def mm_thin(a, b, dims):
    count = a.shape[0]
    rows = split2(a)
    out = bdot(stack(rows, 0), b[0], dims)
    return (out[:count] + out[count:]) + bdot(rows[0], b[1], dims)


def mm_thin6(a, b, dims):
    count = a.shape[0]
    rows = thirds(a)
    one = bdot(stack(rows, 0), b[0], dims)
    two = bdot(stack(rows[:2], 0), b[1], dims)
    small = one[2 * count :] + two[count:] + bdot(rows[0], b[2], dims)
    return one[:count] + (one[count : 2 * count] + two[:count] + small)


def mm_deep(a, b, pairs):
    left = stack([a[i] for i, _ in pairs], 0)
    right = stack([b[j] for _, j in pairs], 0)
    return bdot(left, right, TN)


def sigmoid(x):
    return 1.0 / (1.0 + jnp.exp(-x))


def export_kernel(pos_ref, spec_ref, send_ref, out_ref):
    atoms, count = pos_ref.shape[3], send_ref.shape[2]
    rows = [pos_ref[c, 0] for c in range(3)] + [spec_ref[0].astype(F32)]
    table = jnp.concatenate(rows, axis=0)
    parts = jnp.concatenate(split3(table) + (jnp.zeros_like(table),), axis=0).astype(BF16)
    hot = (iota((atoms, count), 0) == send_ref[0]).astype(F32).astype(BF16)
    found = bdot(parts, hot, NN)
    found = (found[0:4] + found[4:8]) + found[8:12]
    out_ref[...] = jnp.zeros_like(out_ref)
    for j in range(count // LANES):
        for c in range(4):
            out_ref[j : j + 1, c * LANES : (c + 1) * LANES] = found[c : c + 1, j * LANES : (j + 1) * LANES]


def main_kernel(
    side_ref,
    counts_ref,
    pos_ref,
    spec_ref,
    xa_ref,
    xb_ref,
    ya_ref,
    yb_ref,
    cent_ref,
    neigh_ref,
    embc_ref,
    embn_ref,
    radw_ref,
    outw_ref,
    envw_hbm,
    mixw_hbm,
    own_ref,
    a0_ref,
    a1_ref,
    a2_ref,
    pack_ref,
    q_ref,
    w_ref,
    envw_ref,
    mixw_ref,
    sems,
    *,
    blocks,
    devices,
):
    loads = [
        pltpu.make_async_copy(envw_hbm, envw_ref, sems.at[0]),
        pltpu.make_async_copy(mixw_hbm, mixw_ref, sems.at[1]),
    ]
    for load in loads:
        load.start()
    atoms = pos_ref.shape[3]
    edges = cent_ref.shape[2]
    own_rows = atoms // LANES
    side = SPACING * LAT

    for c in range(4):
        row = pos_ref[c, 0] if c < 3 else spec_ref[0].astype(F32)
        for h in range(own_rows):
            q_ref[h : h + 1, c * LANES : (c + 1) * LANES] = row[:, h * LANES : (h + 1) * LANES]
    turn_x = 2 * (side_ref[0] // 2) - 1
    turn_y = 2 * (side_ref[0] % 2) - 1
    lane = iota((4, 4 * LANES), 1)
    for s in range(9):
        a, b = s // 3, s % 3
        rows = slice(own_rows + 4 * s, own_rows + 4 * s + 4)
        if s == 4:
            q_ref[rows, :] = jnp.zeros((4, 4 * LANES), F32)
            continue
        ghost = (ya_ref[a], None, yb_ref[a])[b] if b != 1 else (xa_ref, xb_ref)[a // 2][...]
        shift_x = (turn_x * (a - 1)).astype(F32) * F32(side)
        shift_y = (turn_y * (b - 1)).astype(F32) * F32(side)
        q_ref[rows, :] = ghost + jnp.where(lane < LANES, shift_x, jnp.where(lane < 2 * LANES, shift_y, 0.0))
    total_rows = q_ref.shape[0]

    ends = jnp.concatenate([neigh_ref[0], cent_ref[0]], axis=1)
    at_row = iota((total_rows, 2 * edges), 0)
    past = at_row - own_rows
    slot = 3 * (1 + turn_x * (past // 12 - 1)) + 1 + turn_y * (past // 4 % 3 - 1)
    holds = jnp.where(past < 0, at_row, jnp.where(past % 4 == 3, -1, own_rows + 3 * slot + past % 4))
    hot = (holds == ends // LANES).astype(F32)
    in_lane = iota((LANES, 2 * edges), 0) == ends % LANES
    table = jnp.concatenate(split3(q_ref[...]), axis=0).astype(BF16)
    hot3 = jnp.concatenate([hot, hot, hot], axis=0).astype(BF16)
    runs = bdot(table, hot3, TN)
    picked = [
        jnp.sum(jnp.where(in_lane, runs[c * LANES : (c + 1) * LANES], 0.0), axis=0, keepdims=True) for c in range(4)
    ]

    dist = [p[:, :edges] - p[:, edges:] for p in picked[:3]]
    radius = jnp.sqrt((dist[0] * dist[0] + dist[1] * dist[1] + dist[2] * dist[2]) + SOFTENING)
    inverse = 1.0 / radius
    unit = [d * inverse for d in dist]
    ratio = radius * (1.0 / CUTOFF)
    gap = 1.0 - ratio * ratio
    smooth = gap * gap
    edge = iota((1, edges), 1)
    limit = jnp.full((1, edges), counts_ref[0, 0, 0], jnp.int32)
    for k in range(1, blocks):
        limit = jnp.where(edge >= k * BLOCK_EDGES, counts_ref[0, 0, k], limit)
    live = (edge % BLOCK_EDGES < limit).astype(F32)
    order = (iota((8, edges), 0) + 1).astype(F32) * F32(math.pi / CUTOFF)
    angle = order * radius
    sines, cosines = jnp.sin(angle), jnp.cos(angle)
    basis = sines * inverse
    slope = (order * cosines - basis) * inverse
    kind = iota((8, edges), 0).astype(F32)
    features = jnp.concatenate(
        [
            basis,
            (kind == picked[3][:, edges:]).astype(F32),
            (kind == picked[3][:, :edges]).astype(F32),
        ],
        axis=0,
    )
    species = embc_ref.shape[0]
    w_ref[...] = jnp.zeros_like(w_ref)
    w_ref[0:8, :] = radw_ref[...]
    w_ref[8 : 8 + species, :] = embc_ref[...]
    w_ref[16 : 16 + species, :] = embn_ref[...]

    centre = cent_ref[0].astype(F32)
    weight = live * smooth
    zero = jnp.zeros((1, edges), F32)
    columns = jnp.transpose(jnp.concatenate([smooth, weight, live, centre] + [zero] * 4, axis=0))
    smooth_col, weight_col, live_col, centre_col = (columns[:, k : k + 1] for k in range(4))

    units = jnp.concatenate(unit + [zero] * 5, axis=0)
    units_s = split2(units)
    cosine = mm_deep(units_s, units_s, ((0, 1), (1, 0), (0, 0)))
    same = jnp.logical_and(centre_col == centre, live_col * live > 0.0)
    pairs = split2(jnp.where(same, cosine, 0.0))

    terms = ((0, 2), (1, 1), (2, 0), (0, 1), (1, 0), (0, 0))
    summed = mm_deep(thirds(features), thirds(w_ref[...]), terms)
    gate0 = sigmoid(summed)
    first = summed * gate0
    latent = first * smooth_col

    for load in loads:
        load.wait()
    layers = envw_ref.shape[0]
    chunk = layers * LANES // pack_ref.shape[0]
    share = 1.0 / devices
    saved = []
    for l in range(layers):
        env_s, mix_s = split2(envw_ref[l]), split2(mixw_ref[l])
        weighted_s = split2(mm_square(split2(latent), env_s, NN))
        back = mm_wide(pairs, weighted_s)
        coupled_s = split2(latent * back)
        pre = mm_square(coupled_s, mix_s, NN)
        gate = sigmoid(pre)
        saved.append((env_s, mix_s, weighted_s, latent, back, coupled_s, pre, gate))
        latent = latent + pre * gate

    out_rows = jnp.broadcast_to(outw_ref[...], (8, LANES))
    latent_s = split2(latent)
    readout = mm_thin6(out_rows, thirds(latent), NT)[0:1]
    energy = jnp.sum(weight * readout, axis=1, keepdims=True)
    grad_out = mm_thin(jnp.concatenate([weight] + [zero] * 7, axis=0), latent_s, NN)

    dlatent = weight_col * outw_ref[...]
    lefts, rights = [], []
    for l in reversed(range(layers)):
        env_s, mix_s, weighted_s, latent, back, coupled_s, pre, gate = saved[l]
        dpre_s = split2(dlatent * (gate * (1.0 + pre * (1.0 - gate))))
        grad_mix = mm_turned(coupled_s, dpre_s) * share
        step = min(chunk, LANES)
        for k in range(0, LANES, step):
            place, start = divmod(l * LANES + k, chunk)
            pack_ref[place, start : start + step, :] = grad_mix[k : k + step]
        dcoupled = mm_square(dpre_s, mix_s, NT)
        dback_s = split2(dcoupled * latent)
        lefts += [dback_s[0], dback_s[1], dback_s[0]]
        rights += [weighted_s[0], weighted_s[0], weighted_s[1]]
        dweighted_s = split2(mm_wide(pairs, dback_s))
        dlatent = dlatent + dcoupled * back + mm_square(dweighted_s, env_s, NT)
    row = iota((8, LANES), 0)
    tail = jnp.where(row == 0, grad_out[0:1], jnp.where(row == 1, energy, 0.0)) * share
    for k in range(pack_ref.shape[0]):
        pack_ref[k, chunk:, :] = tail

    dpairs = bdot(jnp.concatenate(lefts, axis=1), jnp.concatenate(rights, axis=1), NT)
    dpairs_s = split2(jnp.where(same, dpairs, 0.0))
    dunits = mm_thin(units, dpairs_s, NT) + mm_thin(units, dpairs_s, NN)
    dfirst_s = split2(dlatent * first)
    ones = jnp.ones((8, LANES), F32).astype(BF16)
    dsmooth = live * readout + (bdot(ones, dfirst_s[0], NT) + bdot(ones, dfirst_s[1], NT))[0:1]
    dsummed = dlatent * smooth_col * (gate0 * (1.0 + summed * (1.0 - gate0)))
    dbasis = mm_thin(w_ref[0:8, :], split2(dsummed), NT)
    dradius = jnp.sum(dbasis * slope, axis=0, keepdims=True) - dsmooth * (gap * radius * F32(4.0 / CUTOFF**2))
    along = dunits[0:1] * unit[0] + dunits[1:2] * unit[1] + dunits[2:3] * unit[2]
    radial = dradius - along * inverse
    units_in = in_lane.astype(F32).astype(BF16)
    hot_b = hot.astype(BF16)
    high, low = [], []
    for c in range(3):
        push = dunits[c : c + 1] * inverse + unit[c] * radial
        for parts, piece in zip((high, low), split2(push)):
            wide = piece.astype(F32)
            parts.append(units_in * jnp.concatenate([wide, -wide], axis=1).astype(BF16))
    pool = bdot(hot_b, jnp.concatenate(high, axis=0), NT) + bdot(hot_b, jnp.concatenate(low, axis=0), NT)
    own_ref[...] = pool[0:own_rows]
    for s in range(9):
        rows = slice(own_rows + 4 * s, own_rows + 4 * s + 4)
        (a0_ref, a1_ref, a2_ref)[s // 3][s % 3] = pool[rows]


def force_kernel(send_ref, own_ref, down_ref, up_ref, left_ref, right_ref, part_ref, out_ref, gout_ref, energy_ref):
    gout_ref[...] = part_ref[0:1, :]
    energy_ref[...] = part_ref[1:2, 0:1]
    atoms, count = out_ref.shape[3], send_ref.shape[2]
    back = (down_ref[1] + up_ref[1]) + (left_ref[...] + right_ref[...])
    rows = []
    for c in range(3):
        lanes = slice(c * LANES, (c + 1) * LANES)
        rows.append(jnp.concatenate([back[j : j + 1, lanes] for j in range(count // LANES)], axis=1))
    rows.append(jnp.zeros((1, count), F32))
    values = jnp.concatenate(rows, axis=0)
    parts = jnp.concatenate(split3(values) + (jnp.zeros_like(values),), axis=0).astype(BF16)
    hot = (iota((atoms, count), 0) == send_ref[0]).astype(F32).astype(BF16)
    placed = bdot(parts, hot, NT)
    placed = (placed[0:4] + placed[4:8]) + placed[8:12]
    own = own_ref[...]
    for c in range(3):
        lanes = slice(c * LANES, (c + 1) * LANES)
        mine = jnp.concatenate([own[h : h + 1, lanes] for h in range(atoms // LANES)], axis=1)
        out_ref[c, 0] = -(mine + placed[c : c + 1])


def traded(block, axis, first):
    count = lax.axis_size(axis)
    route = [(i, (i + 1 if i % 2 == first else i - 1) % count) for i in range(count)]
    return lax.ppermute(block, axis, route)


def exchanged(shard, axes):
    return lax.all_to_all(shard, axes, 0, 0)


def summed_over(shard, axes):
    copies = jnp.broadcast_to(shard[None], (lax.axis_size(axes),) + shard.shape)
    return jnp.sum(exchanged(copies, axes), axis=0)


def body(
    positions,
    species,
    send_index,
    edge_centers,
    edge_neighbours,
    block_counts,
    emb_center,
    emb_neighbour,
    radial_w,
    env_w,
    mix_w,
    out_w,
):
    atoms = positions.shape[3]
    edges = edge_centers.shape[2]
    layers = env_w.shape[0]
    own_rows = atoms // LANES
    devices = lax.axis_size(ALL)
    near = lax.axis_size(NEAR)
    chunk = layers * LANES // near
    vmem = pl.BlockSpec(memory_space=pltpu.VMEM)

    def near_by(*arrays):
        return [pltpu.with_memory_space_constraint(a, pltpu.VMEM) for a in arrays]

    def result(*shape):
        return pltpu.VMEM(shape, F32)

    exported = pl.pallas_call(
        export_kernel,
        out_shape=result(4, 4 * LANES),
        in_specs=[vmem] * 3,
        out_specs=vmem,
        name="export",
    )(positions, species, send_index)

    side = (2 * (lax.axis_index(GX) % 2) + lax.axis_index(GY) % 2).reshape(1)
    xb = traded(exported, GX, 1)
    xa = traded(exported, GX, 0)
    column = jnp.stack([xa, exported, xb])
    yb = traded(column, GY, 1)
    ya = traded(column, GY, 0)

    piece = result(3, 4, 3 * LANES)
    own, a0, a1, a2, pack = pl.pallas_call(
        lambda *refs: main_kernel(*refs, blocks=edges // BLOCK_EDGES, devices=devices),
        out_shape=(
            result(own_rows, 3 * LANES),
            piece,
            piece,
            piece,
            result(near, chunk + 8, LANES),
        ),
        in_specs=[pl.BlockSpec(memory_space=pltpu.SMEM)] * 2 + [vmem] * 12 + [pl.BlockSpec(memory_space=pl.ANY)] * 2,
        out_specs=(vmem,) * 5,
        scratch_shapes=[
            pltpu.VMEM((own_rows + 36, 4 * LANES), F32),
            pltpu.VMEM((24, LANES), F32),
            pltpu.VMEM(env_w.shape, F32),
            pltpu.VMEM(mix_w.shape, F32),
            pltpu.SemaphoreType.DMA((2,)),
        ],
        name="edges",
    )(
        side,
        block_counts,
        *near_by(
            positions,
            species,
            xa,
            xb,
            ya,
            yb,
            edge_centers,
            edge_neighbours,
            emb_center,
            emb_neighbour,
            radial_w,
            out_w.reshape(1, LANES),
        ),
        env_w,
        mix_w,
    )

    over = traded(a2, GX, 1), traded(a0, GX, 0)
    part = jnp.sum(exchanged(pack, NEAR), axis=0)
    part = summed_over(part, MIDDLE)
    part, over = lax.optimization_barrier((part, over))
    across = (
        traded(a1[2] + over[0][2] + over[1][2], GY, 1),
        traded(a1[0] + over[0][0] + over[1][0], GY, 0),
    )
    part = summed_over(part, FAR)
    part, across = lax.optimization_barrier((part, across))
    forces, grad_out, energy = pl.pallas_call(
        force_kernel,
        out_shape=(
            jax.ShapeDtypeStruct(positions.shape, F32),
            jax.ShapeDtypeStruct((1, LANES), F32),
            jax.ShapeDtypeStruct((1, 1), F32),
        ),
        in_specs=[vmem] * 7,
        out_specs=(vmem,) * 3,
        name="forces",
    )(send_index, *near_by(own, *over, *across, part[chunk:]))
    shared = jnp.broadcast_to(part[None, :chunk], (near, chunk, LANES))
    grad_mix = exchanged(shared, NEAR).reshape(layers, LANES, LANES)
    return forces, grad_mix, grad_out.reshape(LANES), energy.reshape(())


def solution(mesh):
    finer = Mesh(mesh.devices.reshape(4, 2, 2, 12, 4), ALL)
    sharded = P(GX, GY, None)
    placed = (P(None, GX, GY, None),) + (sharded,) * 5 + (P(),) * 6
    return jax.shard_map(
        body,
        mesh=finer,
        in_specs=placed,
        out_specs=(P(None, GX, GY, None), P(), P(), P()),
        check_vma=False,
    )
```

```python
import math

import jax
import jax.numpy as jnp
from jax import lax
from jax.experimental import pallas as pl
from jax.experimental.pallas import tpu as pltpu
from jax.sharding import Mesh
from jax.sharding import PartitionSpec as P

BLOCK_EDGES = 128
LAT = 8
CUTOFF = 6.0
SOFTENING = 0.25
SPACING = 1.7
LANES = 128

GX = ("gx_0", "gx_1")
GY = ("gy_0", "gy_1", "gy_2")
ALL = GX + GY
NEAR = ("gx_1", "gy_2")
MIDDLE = ("gx_0", "gy_0")
FAR = ("gy_1",)

F32 = jnp.float32
BF16 = jnp.bfloat16
NN = ((1,), (0,))
NT = ((1,), (1,))
TN = ((0,), (0,))


def iota(shape, dim):
    return lax.broadcasted_iota(jnp.int32, shape, dim)


def bdot(a, b, dims):
    return lax.dot_general(a, b, (dims, ((), ())), preferred_element_type=F32)


def split2(x):
    hi = x.astype(BF16)
    return hi, (x - hi.astype(F32)).astype(BF16)


def split3(x):
    hi = x.astype(BF16).astype(F32)
    rest = x - hi
    mid = rest.astype(BF16).astype(F32)
    return hi, mid, rest - mid


def thirds(x):
    return tuple(part.astype(BF16) for part in split3(x))


def stack(parts, axis):
    return jnp.concatenate([part.astype(F32) for part in parts], axis=axis).astype(BF16)


def halves(out):
    return out[:, :LANES] + out[:, LANES:]


def mm_square(a, b, dims):
    left = jnp.concatenate(a, axis=1)
    if dims == NN:
        row = jnp.concatenate(b, axis=1)
        return halves(bdot(left, jnp.concatenate([row, row], axis=0), NN))
    column = jnp.concatenate(b, axis=0)
    return halves(bdot(left, jnp.concatenate([column, column], axis=1), NT))


def mm_wide(a, b):
    return halves(bdot(a[0], jnp.concatenate(b, axis=1), NN)) + bdot(a[1], b[0], NN)


def mm_turned(a, b):
    out = bdot(jnp.concatenate(a, axis=1), jnp.concatenate(b, axis=1), TN)
    return halves(out[:LANES] + out[LANES:])


def mm_thin(a, b, dims):
    count = a.shape[0]
    rows = split2(a)
    out = bdot(stack(rows, 0), b[0], dims)
    return (out[:count] + out[count:]) + bdot(rows[0], b[1], dims)


def mm_thin6(a, b, dims):
    count = a.shape[0]
    rows = thirds(a)
    one = bdot(stack(rows, 0), b[0], dims)
    two = bdot(stack(rows[:2], 0), b[1], dims)
    small = one[2 * count :] + two[count:] + bdot(rows[0], b[2], dims)
    return one[:count] + (one[count : 2 * count] + two[:count] + small)


def mm_deep(a, b, pairs):
    left = stack([a[i] for i, _ in pairs], 0)
    right = stack([b[j] for _, j in pairs], 0)
    return bdot(left, right, TN)


def sigmoid(x):
    return 1.0 / (1.0 + jnp.exp(-x))


def pool_places(side_ref, neigh_ref, cent_ref, own_rows, total_rows):
    turn_x = 2 * (side_ref[0] // 2) - 1
    turn_y = 2 * (side_ref[0] % 2) - 1
    ends = jnp.concatenate([neigh_ref[0], cent_ref[0]], axis=1)
    count = ends.shape[1]
    at_row = iota((total_rows, count), 0)
    past = at_row - own_rows
    slot = 3 * (1 + turn_x * (past // 12 - 1)) + 1 + turn_y * (past // 4 % 3 - 1)
    holds = jnp.where(past < 0, at_row, jnp.where(past % 4 == 3, -1, own_rows + 3 * slot + past % 4))
    hot = (holds == ends // LANES).astype(F32)
    in_lane = iota((LANES, count), 0) == ends % LANES
    return hot, in_lane


def export_kernel(pos_ref, spec_ref, send_ref, out_ref):
    atoms, count = pos_ref.shape[3], send_ref.shape[2]
    rows = [pos_ref[c, 0] for c in range(3)] + [spec_ref[0].astype(F32)]
    table = jnp.concatenate(rows, axis=0)
    parts = jnp.concatenate(split3(table) + (jnp.zeros_like(table),), axis=0).astype(BF16)
    hot = (iota((atoms, count), 0) == send_ref[0]).astype(F32).astype(BF16)
    found = bdot(parts, hot, NN)
    found = (found[0:4] + found[4:8]) + found[8:12]
    out_ref[...] = jnp.zeros_like(out_ref)
    for j in range(count // LANES):
        for c in range(4):
            out_ref[j : j + 1, c * LANES : (c + 1) * LANES] = found[c : c + 1, j * LANES : (j + 1) * LANES]


def main_kernel(
    side_ref,
    counts_ref,
    pos_ref,
    spec_ref,
    xa_ref,
    xb_ref,
    ya_ref,
    yb_ref,
    cent_ref,
    neigh_ref,
    embc_ref,
    embn_ref,
    radw_ref,
    outw_hbm,
    envw_hbm,
    mixw_hbm,
    pack_ref,
    rows_ref,
    columns_ref,
    pieces_ref,
    drift_ref,
    q_ref,
    w_ref,
    outw_ref,
    envw_ref,
    mixw_ref,
    sems,
    *,
    blocks,
    devices,
):
    loads = [
        pltpu.make_async_copy(envw_hbm, envw_ref, sems.at[0]),
        pltpu.make_async_copy(mixw_hbm, mixw_ref, sems.at[1]),
        pltpu.make_async_copy(outw_hbm, outw_ref, sems.at[2]),
    ]
    for load in loads:
        load.start()
    atoms = pos_ref.shape[3]
    edges = cent_ref.shape[2]
    own_rows = atoms // LANES
    side = SPACING * LAT

    for c in range(4):
        row = pos_ref[c, 0] if c < 3 else spec_ref[0].astype(F32)
        for h in range(own_rows):
            q_ref[h : h + 1, c * LANES : (c + 1) * LANES] = row[:, h * LANES : (h + 1) * LANES]
    turn_x = 2 * (side_ref[0] // 2) - 1
    turn_y = 2 * (side_ref[0] % 2) - 1
    lane = iota((4, 4 * LANES), 1)
    for s in range(9):
        a, b = s // 3, s % 3
        rows = slice(own_rows + 4 * s, own_rows + 4 * s + 4)
        if s == 4:
            q_ref[rows, :] = jnp.zeros((4, 4 * LANES), F32)
            continue
        ghost = (ya_ref[a], None, yb_ref[a])[b] if b != 1 else (xa_ref, xb_ref)[a // 2][...]
        shift_x = (turn_x * (a - 1)).astype(F32) * F32(side)
        shift_y = (turn_y * (b - 1)).astype(F32) * F32(side)
        q_ref[rows, :] = ghost + jnp.where(lane < LANES, shift_x, jnp.where(lane < 2 * LANES, shift_y, 0.0))
    total_rows = q_ref.shape[0]

    hot, in_lane = pool_places(side_ref, neigh_ref, cent_ref, own_rows, total_rows)
    table = jnp.concatenate(split3(q_ref[...]), axis=0).astype(BF16)
    hot3 = jnp.concatenate([hot, hot, hot], axis=0).astype(BF16)
    runs = bdot(table, hot3, TN)
    picked = [
        jnp.sum(jnp.where(in_lane, runs[c * LANES : (c + 1) * LANES], 0.0), axis=0, keepdims=True) for c in range(4)
    ]

    dist = [p[:, :edges] - p[:, edges:] for p in picked[:3]]
    radius = jnp.sqrt((dist[0] * dist[0] + dist[1] * dist[1] + dist[2] * dist[2]) + SOFTENING)
    inverse = 1.0 / radius
    unit = [d * inverse for d in dist]
    ratio = radius * (1.0 / CUTOFF)
    gap = 1.0 - ratio * ratio
    smooth = gap * gap
    edge = iota((1, edges), 1)
    limit = jnp.full((1, edges), counts_ref[0, 0, 0], jnp.int32)
    for k in range(1, blocks):
        limit = jnp.where(edge >= k * BLOCK_EDGES, counts_ref[0, 0, k], limit)
    live = (edge % BLOCK_EDGES < limit).astype(F32)
    order = (iota((8, edges), 0) + 1).astype(F32) * F32(math.pi / CUTOFF)
    angle = order * radius
    sines, cosines = jnp.sin(angle), jnp.cos(angle)
    basis = sines * inverse
    slope = (order * cosines - basis) * inverse
    kind = iota((8, edges), 0).astype(F32)
    features = jnp.concatenate(
        [
            basis,
            (kind == picked[3][:, edges:]).astype(F32),
            (kind == picked[3][:, :edges]).astype(F32),
        ],
        axis=0,
    )
    species = embc_ref.shape[0]
    w_ref[...] = jnp.zeros_like(w_ref)
    w_ref[0:8, :] = radw_ref[...]
    w_ref[8 : 8 + species, :] = embc_ref[...]
    w_ref[16 : 16 + species, :] = embn_ref[...]

    centre = cent_ref[0].astype(F32)
    weight = live * smooth
    zero = jnp.zeros((1, edges), F32)
    columns = jnp.transpose(jnp.concatenate([smooth, weight, live, centre] + [zero] * 4, axis=0))
    columns_ref[...] = columns
    smooth_col, weight_col, live_col, centre_col = (columns[:, k : k + 1] for k in range(4))

    units = jnp.concatenate(unit + [zero] * 5, axis=0)
    units_s = split2(units)
    cosine = mm_deep(units_s, units_s, ((0, 1), (1, 0), (0, 0)))
    same = jnp.logical_and(centre_col == centre, live_col * live > 0.0)
    pairs = split2(jnp.where(same, cosine, 0.0))

    terms = ((0, 2), (1, 1), (2, 0), (0, 1), (1, 0), (0, 0))
    summed = mm_deep(thirds(features), thirds(w_ref[...]), terms)
    gate0 = sigmoid(summed)
    first = summed * gate0
    latent = first * smooth_col

    for load in loads:
        load.wait()
    layers = envw_ref.shape[0]
    chunk = layers * LANES // pack_ref.shape[0]
    share = 1.0 / devices
    saved = []
    for l in range(layers):
        env_s, mix_s = split2(envw_ref[l]), split2(mixw_ref[l])
        weighted_s = split2(mm_square(split2(latent), env_s, NN))
        back = mm_wide(pairs, weighted_s)
        coupled_s = split2(latent * back)
        pre = mm_square(coupled_s, mix_s, NN)
        gate = sigmoid(pre)
        saved.append((env_s, mix_s, weighted_s, latent, back, coupled_s, pre, gate))
        latent = latent + pre * gate

    out_rows = jnp.broadcast_to(outw_ref[...], (8, LANES))
    latent_s = split2(latent)
    readout = mm_thin6(out_rows, thirds(latent), NT)[0:1]
    energy = jnp.sum(weight * readout, axis=1, keepdims=True)
    grad_out = mm_thin(jnp.concatenate([weight] + [zero] * 7, axis=0), latent_s, NN)

    dlatent = weight_col * outw_ref[...]
    for l in reversed(range(layers)):
        env_s, mix_s, weighted_s, latent, back, coupled_s, pre, gate = saved[l]
        dpre_s = split2(dlatent * (gate * (1.0 + pre * (1.0 - gate))))
        grad_mix = mm_turned(coupled_s, dpre_s) * share
        step = min(chunk, LANES)
        for k in range(0, LANES, step):
            place, start = divmod(l * LANES + k, chunk)
            pack_ref[place, start : start + step, :] = grad_mix[k : k + step]
        dcoupled = mm_square(dpre_s, mix_s, NT)
        dback_s = split2(dcoupled * latent)
        for k, piece in enumerate(dback_s + weighted_s):
            pieces_ref[4 * l + k] = piece
        dweighted_s = split2(mm_wide(pairs, dback_s))
        dlatent = dlatent + dcoupled * back + mm_square(dweighted_s, env_s, NT)
    row = iota((8, LANES), 0)
    tail = jnp.where(row == 0, grad_out[0:1], jnp.where(row == 1, energy, 0.0)) * share
    for k in range(pack_ref.shape[0]):
        pack_ref[k, chunk:, :] = tail

    drift_ref[0] = dlatent * first
    drift_ref[1] = dlatent * smooth_col * (gate0 * (1.0 + summed * (1.0 - gate0)))
    rows_ref[0:8, :] = slope
    rows_ref[8:16, :] = jnp.concatenate(unit + [inverse, live, live * readout, gap * radius, centre], axis=0)


def push_kernel(
    side_ref,
    cent_ref,
    neigh_ref,
    radw_ref,
    rows_ref,
    columns_ref,
    pieces_ref,
    drift_ref,
    own_ref,
    a0_ref,
    a1_ref,
    a2_ref,
):
    own_rows = own_ref.shape[0]
    total_rows = own_rows + 36
    edges = cent_ref.shape[2]
    slope = rows_ref[0:8, :]
    unit = [rows_ref[8 + c : 9 + c, :] for c in range(3)]
    inverse, live, lived, widened, centre = (rows_ref[k : k + 1, :] for k in range(11, 16))
    live_col, centre_col = columns_ref[:, 2:3], columns_ref[:, 3:4]
    same = jnp.logical_and(centre_col == centre, live_col * live > 0.0)
    units = jnp.concatenate(unit + [jnp.zeros((1, edges), F32)] * 5, axis=0)
    lefts, rights = [], []
    for l in range(pieces_ref.shape[0] // 4):
        dback_s, weighted_s = (pieces_ref[4 * l], pieces_ref[4 * l + 1]), (pieces_ref[4 * l + 2], pieces_ref[4 * l + 3])
        lefts += [dback_s[0], dback_s[1], dback_s[0]]
        rights += [weighted_s[0], weighted_s[0], weighted_s[1]]
    dpairs = bdot(jnp.concatenate(lefts, axis=1), jnp.concatenate(rights, axis=1), NT)
    dpairs_s = split2(jnp.where(same, dpairs, 0.0))
    dunits = mm_thin(units, dpairs_s, NT) + mm_thin(units, dpairs_s, NN)
    dfirst_s = split2(drift_ref[0])
    ones = jnp.ones((8, LANES), F32).astype(BF16)
    dsmooth = lived + (bdot(ones, dfirst_s[0], NT) + bdot(ones, dfirst_s[1], NT))[0:1]
    dbasis = mm_thin(radw_ref[...], split2(drift_ref[1]), NT)
    dradius = jnp.sum(dbasis * slope, axis=0, keepdims=True) - dsmooth * (widened * F32(4.0 / CUTOFF**2))
    along = dunits[0:1] * unit[0] + dunits[1:2] * unit[1] + dunits[2:3] * unit[2]
    radial = dradius - along * inverse
    hot, in_lane = pool_places(side_ref, neigh_ref, cent_ref, own_rows, total_rows)
    units_in = in_lane.astype(F32).astype(BF16)
    hot_b = hot.astype(BF16)
    high, low = [], []
    for c in range(3):
        push = dunits[c : c + 1] * inverse + unit[c] * radial
        for parts, piece in zip((high, low), split2(push)):
            wide = piece.astype(F32)
            parts.append(units_in * jnp.concatenate([wide, -wide], axis=1).astype(BF16))
    pool = bdot(hot_b, jnp.concatenate(high, axis=0), NT) + bdot(hot_b, jnp.concatenate(low, axis=0), NT)
    own_ref[...] = pool[0:own_rows]
    for s in range(9):
        rows = slice(own_rows + 4 * s, own_rows + 4 * s + 4)
        (a0_ref, a1_ref, a2_ref)[s // 3][s % 3] = pool[rows]


def force_kernel(send_ref, own_ref, down_ref, up_ref, left_ref, right_ref, part_ref, out_ref, gout_ref, energy_ref):
    gout_ref[...] = part_ref[0:1, :]
    energy_ref[...] = part_ref[1:2, 0:1]
    atoms, count = out_ref.shape[3], send_ref.shape[2]
    back = (down_ref[1] + up_ref[1]) + (left_ref[...] + right_ref[...])
    rows = []
    for c in range(3):
        lanes = slice(c * LANES, (c + 1) * LANES)
        rows.append(jnp.concatenate([back[j : j + 1, lanes] for j in range(count // LANES)], axis=1))
    rows.append(jnp.zeros((1, count), F32))
    values = jnp.concatenate(rows, axis=0)
    parts = jnp.concatenate(split3(values) + (jnp.zeros_like(values),), axis=0).astype(BF16)
    hot = (iota((atoms, count), 0) == send_ref[0]).astype(F32).astype(BF16)
    placed = bdot(parts, hot, NT)
    placed = (placed[0:4] + placed[4:8]) + placed[8:12]
    own = own_ref[...]
    for c in range(3):
        lanes = slice(c * LANES, (c + 1) * LANES)
        mine = jnp.concatenate([own[h : h + 1, lanes] for h in range(atoms // LANES)], axis=1)
        out_ref[c, 0] = -(mine + placed[c : c + 1])


def traded(block, axis, first):
    count = lax.axis_size(axis)
    route = [(i, (i + 1 if i % 2 == first else i - 1) % count) for i in range(count)]
    return lax.ppermute(block, axis, route)


def sum_kernel(in_ref, *out_refs):
    total = in_ref[0]
    for k in range(1, in_ref.shape[0]):
        total = total + in_ref[k]
    rows = out_refs[0].shape[1]
    for k in range(out_refs[0].shape[0]):
        out_refs[0][k] = total[:rows]
    if len(out_refs) > 1:
        out_refs[1][...] = total[rows:]


def summed(copies, *shapes):
    vmem = pl.BlockSpec(memory_space=pltpu.VMEM)
    return pl.pallas_call(
        sum_kernel,
        out_shape=tuple(pltpu.VMEM(shape, F32) for shape in shapes),
        in_specs=[vmem],
        out_specs=(vmem,) * len(shapes),
        name="sums",
    )(pltpu.with_memory_space_constraint(copies, pltpu.VMEM))


def exchanged(shard, axes):
    return lax.all_to_all(shard, axes, 0, 0)


def body(
    positions,
    species,
    send_index,
    edge_centers,
    edge_neighbours,
    block_counts,
    emb_center,
    emb_neighbour,
    radial_w,
    env_w,
    mix_w,
    out_w,
):
    atoms = positions.shape[3]
    edges = edge_centers.shape[2]
    layers = env_w.shape[0]
    own_rows = atoms // LANES
    devices = lax.axis_size(ALL)
    near = lax.axis_size(NEAR)
    chunk = layers * LANES // near
    vmem = pl.BlockSpec(memory_space=pltpu.VMEM)

    def near_by(*arrays):
        return [pltpu.with_memory_space_constraint(a, pltpu.VMEM) for a in arrays]

    def result(*shape):
        return pltpu.VMEM(shape, F32)

    exported = pl.pallas_call(
        export_kernel,
        out_shape=result(4, 4 * LANES),
        in_specs=[vmem] * 3,
        out_specs=vmem,
        name="export",
    )(positions, species, send_index)

    side = (2 * (lax.axis_index(GX) % 2) + lax.axis_index(GY) % 2).reshape(1)
    xb = traded(exported, GX, 1)
    xa = traded(exported, GX, 0)
    column = jnp.stack([xa, exported, xb])
    yb = traded(column, GY, 1)
    ya = traded(column, GY, 0)

    piece = result(3, 4, 3 * LANES)
    scalars = pl.BlockSpec(memory_space=pltpu.SMEM)
    anywhere = pl.BlockSpec(memory_space=pl.ANY)
    pack, *kept = pl.pallas_call(
        lambda *refs: main_kernel(*refs, blocks=edges // BLOCK_EDGES, devices=devices),
        out_shape=(
            result(near, chunk + 8, LANES),
            result(16, edges),
            result(edges, 8),
            pltpu.VMEM((4 * layers, edges, LANES), BF16),
            result(2, edges, LANES),
        ),
        in_specs=[scalars] * 2 + [vmem] * 11 + [anywhere] * 3,
        out_specs=(vmem,) * 5,
        scratch_shapes=[
            pltpu.VMEM((own_rows + 36, 4 * LANES), F32),
            pltpu.VMEM((24, LANES), F32),
            pltpu.VMEM((1, LANES), F32),
            pltpu.VMEM(env_w.shape, F32),
            pltpu.VMEM(mix_w.shape, F32),
            pltpu.SemaphoreType.DMA((3,)),
        ],
        name="edges",
    )(
        side,
        block_counts,
        *near_by(
            positions,
            species,
            xa,
            xb,
            ya,
            yb,
            edge_centers,
            edge_neighbours,
            emb_center,
            emb_neighbour,
            radial_w,
        ),
        out_w.reshape(1, LANES),
        env_w,
        mix_w,
    )
    parts = exchanged(pack, NEAR)
    own, a0, a1, a2 = pl.pallas_call(
        push_kernel,
        out_shape=(result(own_rows, 3 * LANES), piece, piece, piece),
        in_specs=[scalars] + [vmem] * 7,
        out_specs=(vmem,) * 4,
        cost_estimate=pl.CostEstimate(flops=1_000_000_000, bytes_accessed=2_000_000, transcendentals=0),
        name="pushes",
    )(side, *near_by(edge_centers, edge_neighbours, radial_w, *kept))

    parts, own, a0, a1, a2 = lax.optimization_barrier((parts, own, a0, a1, a2))
    (copies,) = summed(parts, (lax.axis_size(MIDDLE), chunk + 8, LANES))
    over = traded(a2, GX, 1), traded(a0, GX, 0)
    (copies,) = summed(exchanged(copies, MIDDLE), (lax.axis_size(FAR), chunk + 8, LANES))
    copies, over = lax.optimization_barrier((copies, over))
    across = (
        traded(a1[2] + over[0][2] + over[1][2], GY, 1),
        traded(a1[0] + over[0][0] + over[1][0], GY, 0),
    )
    parts = exchanged(copies, FAR)
    parts, across = lax.optimization_barrier((parts, across))
    shared, rest = summed(parts, (near, chunk, LANES), (8, LANES))
    forces, grad_out, energy = pl.pallas_call(
        force_kernel,
        out_shape=(
            jax.ShapeDtypeStruct(positions.shape, F32),
            jax.ShapeDtypeStruct((1, LANES), F32),
            jax.ShapeDtypeStruct((1, 1), F32),
        ),
        in_specs=[vmem] * 7,
        out_specs=(vmem,) * 3,
        name="forces",
    )(send_index, *near_by(own, *over, *across, rest))
    grad_mix = exchanged(shared, NEAR).reshape(layers, LANES, LANES)
    return forces, grad_mix, grad_out.reshape(LANES), energy.reshape(())


def solution(mesh):
    finer = Mesh(mesh.devices.reshape(4, 2, 2, 12, 4), ALL)
    sharded = P(GX, GY, None)
    placed = (P(None, GX, GY, None),) + (sharded,) * 5 + (P(),) * 6
    return jax.shard_map(
        body,
        mesh=finer,
        in_specs=placed,
        out_specs=(P(None, GX, GY, None), P(), P(), P()),
        check_vma=False,
    )
```

```python
import math

import jax
import jax.numpy as jnp
from jax import lax
from jax.experimental import pallas as pl
from jax.experimental.pallas import tpu as pltpu
from jax.sharding import Mesh
from jax.sharding import PartitionSpec as P

BLOCK_EDGES = 128
LAT = 8
CUTOFF = 6.0
SOFTENING = 0.25
SPACING = 1.7
LANES = 128

GX = ("gx_0", "gx_1")
GY = ("gy_0", "gy_1", "gy_2")
ALL = GX + GY
NEAR = ("gx_1", "gy_2")
MIDDLE = ("gx_0", "gy_0")
FAR = ("gy_1",)

F32 = jnp.float32
BF16 = jnp.bfloat16
NN = ((1,), (0,))
NT = ((1,), (1,))
TN = ((0,), (0,))


def iota(shape, dim):
    return lax.broadcasted_iota(jnp.int32, shape, dim)


def bdot(a, b, dims):
    return lax.dot_general(a, b, (dims, ((), ())), preferred_element_type=F32)


def split2(x):
    hi = x.astype(BF16)
    return hi, (x - hi.astype(F32)).astype(BF16)


def split3(x):
    hi = x.astype(BF16).astype(F32)
    rest = x - hi
    mid = rest.astype(BF16).astype(F32)
    return hi, mid, rest - mid


def thirds(x):
    return tuple(part.astype(BF16) for part in split3(x))


def stack(parts, axis):
    return jnp.concatenate([part.astype(F32) for part in parts], axis=axis).astype(BF16)


def halves(out):
    return out[:, :LANES] + out[:, LANES:]


def mm_square(a, b, dims):
    left = jnp.concatenate(a, axis=1)
    if dims == NN:
        row = jnp.concatenate(b, axis=1)
        return halves(bdot(left, jnp.concatenate([row, row], axis=0), NN))
    column = jnp.concatenate(b, axis=0)
    return halves(bdot(left, jnp.concatenate([column, column], axis=1), NT))


def mm_wide(a, b):
    return halves(bdot(a[0], jnp.concatenate(b, axis=1), NN)) + bdot(a[1], b[0], NN)


def mm_turned(a, b):
    out = bdot(jnp.concatenate(a, axis=1), jnp.concatenate(b, axis=1), TN)
    return halves(out[:LANES] + out[LANES:])


def mm_thin(a, b, dims):
    count = a.shape[0]
    rows = split2(a)
    out = bdot(stack(rows, 0), b[0], dims)
    return (out[:count] + out[count:]) + bdot(rows[0], b[1], dims)


def mm_thin6(a, b, dims):
    count = a.shape[0]
    rows = thirds(a)
    one = bdot(stack(rows, 0), b[0], dims)
    two = bdot(stack(rows[:2], 0), b[1], dims)
    small = one[2 * count :] + two[count:] + bdot(rows[0], b[2], dims)
    return one[:count] + (one[count : 2 * count] + two[:count] + small)


def mm_deep(a, b, pairs):
    left = stack([a[i] for i, _ in pairs], 0)
    right = stack([b[j] for _, j in pairs], 0)
    return bdot(left, right, TN)


def sigmoid(x):
    return 1.0 / (1.0 + jnp.exp(-x))


def pool_places(side_ref, neigh_ref, cent_ref, own_rows, total_rows):
    turn_x = 2 * (side_ref[0] // 2) - 1
    turn_y = 2 * (side_ref[0] % 2) - 1
    ends = jnp.concatenate([neigh_ref[0], cent_ref[0]], axis=1)
    count = ends.shape[1]
    at_row = iota((total_rows, count), 0)
    past = at_row - own_rows
    slot = 3 * (1 + turn_x * (past // 12 - 1)) + 1 + turn_y * (past // 4 % 3 - 1)
    holds = jnp.where(past < 0, at_row, jnp.where(past % 4 == 3, -1, own_rows + 3 * slot + past % 4))
    hot = (holds == ends // LANES).astype(F32)
    in_lane = iota((LANES, count), 0) == ends % LANES
    return hot, in_lane


def export_kernel(pos_ref, spec_ref, send_ref, out_ref):
    atoms, count = pos_ref.shape[3], send_ref.shape[2]
    rows = [pos_ref[c, 0] for c in range(3)] + [spec_ref[0].astype(F32)]
    table = jnp.concatenate(rows, axis=0)
    parts = jnp.concatenate(split3(table) + (jnp.zeros_like(table),), axis=0).astype(BF16)
    hot = (iota((atoms, count), 0) == send_ref[0]).astype(F32).astype(BF16)
    found = bdot(parts, hot, NN)
    found = (found[0:4] + found[4:8]) + found[8:12]
    out_ref[...] = jnp.zeros_like(out_ref)
    for j in range(count // LANES):
        for c in range(4):
            out_ref[j : j + 1, c * LANES : (c + 1) * LANES] = found[c : c + 1, j * LANES : (j + 1) * LANES]


def main_kernel(
    side_ref,
    counts_ref,
    pos_ref,
    spec_ref,
    xa_ref,
    xb_ref,
    ya_ref,
    yb_ref,
    cent_ref,
    neigh_ref,
    embc_ref,
    embn_ref,
    radw_ref,
    outw_hbm,
    envw_hbm,
    mixw_hbm,
    pack_ref,
    rows_ref,
    columns_ref,
    pieces_ref,
    drift_ref,
    q_ref,
    w_ref,
    outw_ref,
    envw_ref,
    mixw_ref,
    sems,
    *,
    blocks,
    devices,
):
    loads = [
        pltpu.make_async_copy(envw_hbm, envw_ref, sems.at[0]),
        pltpu.make_async_copy(mixw_hbm, mixw_ref, sems.at[1]),
        pltpu.make_async_copy(outw_hbm, outw_ref, sems.at[2]),
    ]
    for load in loads:
        load.start()
    atoms = pos_ref.shape[3]
    edges = cent_ref.shape[2]
    own_rows = atoms // LANES
    side = SPACING * LAT

    for c in range(4):
        row = pos_ref[c, 0] if c < 3 else spec_ref[0].astype(F32)
        for h in range(own_rows):
            q_ref[h : h + 1, c * LANES : (c + 1) * LANES] = row[:, h * LANES : (h + 1) * LANES]
    turn_x = 2 * (side_ref[0] // 2) - 1
    turn_y = 2 * (side_ref[0] % 2) - 1
    lane = iota((4, 4 * LANES), 1)
    for s in range(9):
        a, b = s // 3, s % 3
        rows = slice(own_rows + 4 * s, own_rows + 4 * s + 4)
        if s == 4:
            q_ref[rows, :] = jnp.zeros((4, 4 * LANES), F32)
            continue
        ghost = (ya_ref[a], None, yb_ref[a])[b] if b != 1 else (xa_ref, xb_ref)[a // 2][...]
        shift_x = (turn_x * (a - 1)).astype(F32) * F32(side)
        shift_y = (turn_y * (b - 1)).astype(F32) * F32(side)
        q_ref[rows, :] = ghost + jnp.where(lane < LANES, shift_x, jnp.where(lane < 2 * LANES, shift_y, 0.0))
    total_rows = q_ref.shape[0]

    hot, in_lane = pool_places(side_ref, neigh_ref, cent_ref, own_rows, total_rows)
    table = jnp.concatenate(split3(q_ref[...]), axis=0).astype(BF16)
    hot3 = jnp.concatenate([hot, hot, hot], axis=0).astype(BF16)
    runs = bdot(table, hot3, TN)
    picked = [
        jnp.sum(jnp.where(in_lane, runs[c * LANES : (c + 1) * LANES], 0.0), axis=0, keepdims=True) for c in range(4)
    ]

    dist = [p[:, :edges] - p[:, edges:] for p in picked[:3]]
    radius = jnp.sqrt((dist[0] * dist[0] + dist[1] * dist[1] + dist[2] * dist[2]) + SOFTENING)
    inverse = 1.0 / radius
    unit = [d * inverse for d in dist]
    ratio = radius * (1.0 / CUTOFF)
    gap = 1.0 - ratio * ratio
    smooth = gap * gap
    edge = iota((1, edges), 1)
    limit = jnp.full((1, edges), counts_ref[0, 0, 0], jnp.int32)
    for k in range(1, blocks):
        limit = jnp.where(edge >= k * BLOCK_EDGES, counts_ref[0, 0, k], limit)
    live = (edge % BLOCK_EDGES < limit).astype(F32)
    order = (iota((8, edges), 0) + 1).astype(F32) * F32(math.pi / CUTOFF)
    angle = order * radius
    sines, cosines = jnp.sin(angle), jnp.cos(angle)
    basis = sines * inverse
    slope = (order * cosines - basis) * inverse
    kind = iota((8, edges), 0).astype(F32)
    features = jnp.concatenate(
        [
            basis,
            (kind == picked[3][:, edges:]).astype(F32),
            (kind == picked[3][:, :edges]).astype(F32),
        ],
        axis=0,
    )
    species = embc_ref.shape[0]
    w_ref[...] = jnp.zeros_like(w_ref)
    w_ref[0:8, :] = radw_ref[...]
    w_ref[8 : 8 + species, :] = embc_ref[...]
    w_ref[16 : 16 + species, :] = embn_ref[...]

    centre = cent_ref[0].astype(F32)
    weight = live * smooth
    zero = jnp.zeros((1, edges), F32)
    columns = jnp.transpose(jnp.concatenate([smooth, weight, live, centre] + [zero] * 4, axis=0))
    columns_ref[...] = columns
    smooth_col, weight_col, live_col, centre_col = (columns[:, k : k + 1] for k in range(4))

    units = jnp.concatenate(unit + [zero] * 5, axis=0)
    units_s = split2(units)
    cosine = mm_deep(units_s, units_s, ((0, 1), (1, 0), (0, 0)))
    same = jnp.logical_and(centre_col == centre, live_col * live > 0.0)
    pairs = split2(jnp.where(same, cosine, 0.0))

    terms = ((0, 2), (1, 1), (2, 0), (0, 1), (1, 0), (0, 0))
    summed = mm_deep(thirds(features), thirds(w_ref[...]), terms)
    gate0 = sigmoid(summed)
    first = summed * gate0
    latent = first * smooth_col

    for load in loads:
        load.wait()
    layers = envw_ref.shape[0]
    chunk = layers * LANES // pack_ref.shape[0]
    share = 1.0 / devices
    saved = []
    for l in range(layers):
        env_s, mix_s = split2(envw_ref[l]), split2(mixw_ref[l])
        weighted_s = split2(mm_square(split2(latent), env_s, NN))
        back = mm_wide(pairs, weighted_s)
        coupled_s = split2(latent * back)
        pre = mm_square(coupled_s, mix_s, NN)
        gate = sigmoid(pre)
        saved.append((env_s, mix_s, weighted_s, latent, back, coupled_s, pre, gate))
        latent = latent + pre * gate

    out_rows = jnp.broadcast_to(outw_ref[...], (8, LANES))
    latent_s = split2(latent)
    readout = mm_thin6(out_rows, thirds(latent), NT)[0:1]
    energy = jnp.sum(weight * readout, axis=1, keepdims=True)
    grad_out = mm_thin(jnp.concatenate([weight] + [zero] * 7, axis=0), latent_s, NN)

    dlatent = weight_col * outw_ref[...]
    for l in reversed(range(layers)):
        env_s, mix_s, weighted_s, latent, back, coupled_s, pre, gate = saved[l]
        dpre_s = split2(dlatent * (gate * (1.0 + pre * (1.0 - gate))))
        grad_mix = mm_turned(coupled_s, dpre_s) * share
        for k in range(LANES):
            place, q = divmod(l * LANES + k, chunk)
            row, run = divmod(q, chunk // 4)
            pack_ref[place, row : row + 1, run * LANES : (run + 1) * LANES] = grad_mix[k : k + 1]
        dcoupled = mm_square(dpre_s, mix_s, NT)
        dback_s = split2(dcoupled * latent)
        for k, piece in enumerate(dback_s + weighted_s):
            pieces_ref[4 * l + k] = piece
        dweighted_s = split2(mm_wide(pairs, dback_s))
        dlatent = dlatent + dcoupled * back + mm_square(dweighted_s, env_s, NT)
    row = iota((8, LANES), 0)
    tail = jnp.where(row == 0, grad_out[0:1], jnp.where(row == 1, energy, 0.0)) * share
    for k in range(pack_ref.shape[0]):
        pack_ref[k, :, chunk // 4 * LANES :] = tail[0:4]

    drift_ref[0] = dlatent * first
    drift_ref[1] = dlatent * smooth_col * (gate0 * (1.0 + summed * (1.0 - gate0)))
    rows_ref[0:8, :] = slope
    rows_ref[8:16, :] = jnp.concatenate(unit + [inverse, live, live * readout, gap * radius, centre], axis=0)


def push_kernel(
    side_ref,
    cent_ref,
    neigh_ref,
    radw_ref,
    rows_ref,
    columns_ref,
    pieces_ref,
    drift_ref,
    own_ref,
    a0_ref,
    a1_ref,
    a2_ref,
):
    own_rows = own_ref.shape[0]
    total_rows = own_rows + 36
    edges = cent_ref.shape[2]
    slope = rows_ref[0:8, :]
    unit = [rows_ref[8 + c : 9 + c, :] for c in range(3)]
    inverse, live, lived, widened, centre = (rows_ref[k : k + 1, :] for k in range(11, 16))
    live_col, centre_col = columns_ref[:, 2:3], columns_ref[:, 3:4]
    same = jnp.logical_and(centre_col == centre, live_col * live > 0.0)
    units = jnp.concatenate(unit + [jnp.zeros((1, edges), F32)] * 5, axis=0)
    lefts, rights = [], []
    for l in range(pieces_ref.shape[0] // 4):
        dback_s, weighted_s = (pieces_ref[4 * l], pieces_ref[4 * l + 1]), (pieces_ref[4 * l + 2], pieces_ref[4 * l + 3])
        lefts += [dback_s[0], dback_s[1], dback_s[0]]
        rights += [weighted_s[0], weighted_s[0], weighted_s[1]]
    dpairs = bdot(jnp.concatenate(lefts, axis=1), jnp.concatenate(rights, axis=1), NT)
    dpairs_s = split2(jnp.where(same, dpairs, 0.0))
    dunits = mm_thin(units, dpairs_s, NT) + mm_thin(units, dpairs_s, NN)
    dfirst_s = split2(drift_ref[0])
    ones = jnp.ones((8, LANES), F32).astype(BF16)
    dsmooth = lived + (bdot(ones, dfirst_s[0], NT) + bdot(ones, dfirst_s[1], NT))[0:1]
    dbasis = mm_thin(radw_ref[...], split2(drift_ref[1]), NT)
    dradius = jnp.sum(dbasis * slope, axis=0, keepdims=True) - dsmooth * (widened * F32(4.0 / CUTOFF**2))
    along = dunits[0:1] * unit[0] + dunits[1:2] * unit[1] + dunits[2:3] * unit[2]
    radial = dradius - along * inverse
    hot, in_lane = pool_places(side_ref, neigh_ref, cent_ref, own_rows, total_rows)
    units_in = in_lane.astype(F32).astype(BF16)
    hot_b = hot.astype(BF16)
    high, low = [], []
    for c in range(3):
        push = dunits[c : c + 1] * inverse + unit[c] * radial
        for parts, piece in zip((high, low), split2(push)):
            wide = piece.astype(F32)
            parts.append(units_in * jnp.concatenate([wide, -wide], axis=1).astype(BF16))
    pool = bdot(hot_b, jnp.concatenate(high, axis=0), NT) + bdot(hot_b, jnp.concatenate(low, axis=0), NT)
    own_ref[...] = pool[0:own_rows]
    for s in range(9):
        rows = slice(own_rows + 4 * s, own_rows + 4 * s + 4)
        (a0_ref, a1_ref, a2_ref)[s // 3][s % 3] = pool[rows]


def force_kernel(send_ref, own_ref, down_ref, up_ref, left_ref, right_ref, part_ref, out_ref, gout_ref, energy_ref):
    gout_ref[...] = part_ref[0:1, :]
    energy_ref[...] = part_ref[1:2, 0:1]
    atoms, count = out_ref.shape[3], send_ref.shape[2]
    back = (down_ref[1] + up_ref[1]) + (left_ref[...] + right_ref[...])
    rows = []
    for c in range(3):
        lanes = slice(c * LANES, (c + 1) * LANES)
        rows.append(jnp.concatenate([back[j : j + 1, lanes] for j in range(count // LANES)], axis=1))
    rows.append(jnp.zeros((1, count), F32))
    values = jnp.concatenate(rows, axis=0)
    parts = jnp.concatenate(split3(values) + (jnp.zeros_like(values),), axis=0).astype(BF16)
    hot = (iota((atoms, count), 0) == send_ref[0]).astype(F32).astype(BF16)
    placed = bdot(parts, hot, NT)
    placed = (placed[0:4] + placed[4:8]) + placed[8:12]
    own = own_ref[...]
    for c in range(3):
        lanes = slice(c * LANES, (c + 1) * LANES)
        mine = jnp.concatenate([own[h : h + 1, lanes] for h in range(atoms // LANES)], axis=1)
        out_ref[c, 0] = -(mine + placed[c : c + 1])


def traded(block, axis, first):
    count = lax.axis_size(axis)
    route = [(i, (i + 1 if i % 2 == first else i - 1) % count) for i in range(count)]
    return lax.ppermute(block, axis, route)


def sum_kernel(in_ref, *out_refs):
    total = in_ref[0]
    for k in range(1, in_ref.shape[0]):
        total = total + in_ref[k]
    first = total
    if len(out_refs) > 1:
        runs = out_refs[0].shape[1] // 4
        first = jnp.concatenate(
            [total[r : r + 1, k * LANES : (k + 1) * LANES] for r in range(4) for k in range(runs)], axis=0
        )
        out_refs[1][...] = total[:, runs * LANES :]
    for k in range(out_refs[0].shape[0]):
        out_refs[0][k] = first


def summed(copies, *shapes):
    vmem = pl.BlockSpec(memory_space=pltpu.VMEM)
    return pl.pallas_call(
        sum_kernel,
        out_shape=tuple(pltpu.VMEM(shape, F32) for shape in shapes),
        in_specs=[vmem],
        out_specs=(vmem,) * len(shapes),
        name="sums",
    )(pltpu.with_memory_space_constraint(copies, pltpu.VMEM))


def exchanged(shard, axes):
    return lax.all_to_all(shard, axes, 0, 0)


def body(
    positions,
    species,
    send_index,
    edge_centers,
    edge_neighbours,
    block_counts,
    emb_center,
    emb_neighbour,
    radial_w,
    env_w,
    mix_w,
    out_w,
):
    atoms = positions.shape[3]
    edges = edge_centers.shape[2]
    layers = env_w.shape[0]
    own_rows = atoms // LANES
    devices = lax.axis_size(ALL)
    near = lax.axis_size(NEAR)
    chunk = layers * LANES // near
    vmem = pl.BlockSpec(memory_space=pltpu.VMEM)

    def near_by(*arrays):
        return [pltpu.with_memory_space_constraint(a, pltpu.VMEM) for a in arrays]

    def result(*shape):
        return pltpu.VMEM(shape, F32)

    exported = pl.pallas_call(
        export_kernel,
        out_shape=result(4, 4 * LANES),
        in_specs=[vmem] * 3,
        out_specs=vmem,
        name="export",
    )(positions, species, send_index)

    side = (2 * (lax.axis_index(GX) % 2) + lax.axis_index(GY) % 2).reshape(1)
    xb = traded(exported, GX, 1)
    xa = traded(exported, GX, 0)
    column = jnp.stack([xa, exported, xb])
    yb = traded(column, GY, 1)
    ya = traded(column, GY, 0)

    piece = result(3, 4, 3 * LANES)
    scalars = pl.BlockSpec(memory_space=pltpu.SMEM)
    anywhere = pl.BlockSpec(memory_space=pl.ANY)
    pack, *kept = pl.pallas_call(
        lambda *refs: main_kernel(*refs, blocks=edges // BLOCK_EDGES, devices=devices),
        out_shape=(
            result(near, 4, (chunk // 4 + 1) * LANES),
            result(16, edges),
            result(edges, 8),
            pltpu.VMEM((4 * layers, edges, LANES), BF16),
            result(2, edges, LANES),
        ),
        in_specs=[scalars] * 2 + [vmem] * 11 + [anywhere] * 3,
        out_specs=(vmem,) * 5,
        scratch_shapes=[
            pltpu.VMEM((own_rows + 36, 4 * LANES), F32),
            pltpu.VMEM((24, LANES), F32),
            pltpu.VMEM((1, LANES), F32),
            pltpu.VMEM(env_w.shape, F32),
            pltpu.VMEM(mix_w.shape, F32),
            pltpu.SemaphoreType.DMA((3,)),
        ],
        name="edges",
    )(
        side,
        block_counts,
        *near_by(
            positions,
            species,
            xa,
            xb,
            ya,
            yb,
            edge_centers,
            edge_neighbours,
            emb_center,
            emb_neighbour,
            radial_w,
        ),
        out_w.reshape(1, LANES),
        env_w,
        mix_w,
    )
    parts = exchanged(pack, NEAR)
    own, a0, a1, a2 = pl.pallas_call(
        push_kernel,
        out_shape=(result(own_rows, 3 * LANES), piece, piece, piece),
        in_specs=[scalars] + [vmem] * 7,
        out_specs=(vmem,) * 4,
        cost_estimate=pl.CostEstimate(flops=1_000_000_000, bytes_accessed=2_000_000, transcendentals=0),
        name="pushes",
    )(side, *near_by(edge_centers, edge_neighbours, radial_w, *kept))

    parts, own, a0, a1, a2 = lax.optimization_barrier((parts, own, a0, a1, a2))
    (copies,) = summed(parts, (lax.axis_size(MIDDLE),) + pack.shape[1:])
    over = traded(a2, GX, 1), traded(a0, GX, 0)
    (copies,) = summed(exchanged(copies, MIDDLE), (lax.axis_size(FAR),) + pack.shape[1:])
    copies, over = lax.optimization_barrier((copies, over))
    across = (
        traded(a1[2] + over[0][2] + over[1][2], GY, 1),
        traded(a1[0] + over[0][0] + over[1][0], GY, 0),
    )
    parts = exchanged(copies, FAR)
    parts, across = lax.optimization_barrier((parts, across))
    shared, rest = summed(parts, (near, chunk, LANES), (4, LANES))
    forces, grad_out, energy = pl.pallas_call(
        force_kernel,
        out_shape=(
            jax.ShapeDtypeStruct(positions.shape, F32),
            jax.ShapeDtypeStruct((1, LANES), F32),
            jax.ShapeDtypeStruct((1, 1), F32),
        ),
        in_specs=[vmem] * 7,
        out_specs=(vmem,) * 3,
        name="forces",
    )(send_index, *near_by(own, *over, *across, rest))
    grad_mix = exchanged(shared, NEAR).reshape(layers, LANES, LANES)
    return forces, grad_mix, grad_out.reshape(LANES), energy.reshape(())


def solution(mesh):
    finer = Mesh(mesh.devices.reshape(4, 2, 2, 12, 4), ALL)
    sharded = P(GX, GY, None)
    placed = (P(None, GX, GY, None),) + (sharded,) * 5 + (P(),) * 6
    return jax.shard_map(
        body,
        mesh=finer,
        in_specs=placed,
        out_specs=(P(None, GX, GY, None), P(), P(), P()),
        check_vma=False,
    )
```
